32 devices in a mesh: phase: 16 (over z, y, x), lat: 2 (over core).
Axes of the slice: x: 2, y: 2, z: 4, core: 2. Of those that a mesh axis runs over, the one named last changes fastest.
Arguments:
- state_now: float32 [3, 64, 1024], P(None, ('lat', 'phase')), may hold values from -4 to 4
- ocean_depth: float32 [64, 1024], P('lat'), may hold values from 0.5 to 1.5
- coriolis: float32 [64], P('lat'), may hold values from -0.4 to 0.4
- phase_times: float32 [16], P('phase'), may hold values from -6 to 6
- phase_weights: float32 [16], P('phase'), may hold values from 0.00625 to 0.25
Outputs:
- state_next: float32 [3, 64, 1024], P(None, ('lat', 'phase'))
- tendency: float32 [3, 64, 1024], P(None, ('lat', 'phase'))
The draws below stay inside these ranges and needn't reach their ends.
All inputs are finite; a program needn't handle non-finite values.
Results may differ from the reference program's by a relative error of at most 0.00002.
Values sent between devices are 32-bit elements; how exact they have to be, the bound alone decides.
A program may use at most 64 MiB of HBM per device.

```python
import math
import jax
import jax.numpy as jnp
from jax import lax

NLON = 1024
DEG = 8
NLAT = 64
SAMPLES = 16


def steps_of(stream_key, dims, split, least, top_value):
    factor_of, own = 1.0, jax.random.fold_in(stream_key, 6)
    for axis_at, parts in split:
        steps = jnp.exp(jax.random.uniform(jax.random.fold_in(own, axis_at), (parts,), jnp.float32, least / len(split), top_value / len(split)))
        factor_of = factor_of * jnp.repeat(steps, dims[axis_at] // parts).reshape([-1 if axis == axis_at else 1 for axis in range(len(dims))])
    return factor_of


def gaussian(stream_key, shape, deviation, most, pieces=(), held_as=jnp.bfloat16):
    level = steps_of(stream_key, shape, pieces, -0.22, 0.18) if pieces else 1.0
    array = jax.random.normal(stream_key, shape, jnp.float32) * deviation * level
    return jnp.minimum(jnp.maximum(array, -most), most).astype(held_as)


def setup_inputs(seed: int = 0) -> dict:
    streams_of = jax.random.split(jax.random.key(seed), 6)
    return {
        "state_now": gaussian(streams_of[0], (3, NLAT, NLON), 1.0, 4.0, ((1, 32),), jnp.float32),
        "ocean_depth": jnp.clip(0.5 + 1.0 * jax.random.uniform(streams_of[1], (NLAT, NLON), jnp.float32) ** steps_of(streams_of[1], (NLAT, NLON), ((0, 2),), -0.2, 0.2), 0.5, 1.5),
        "coriolis": jnp.clip(jax.random.uniform(streams_of[2], (NLAT,), jnp.float32, -0.4, 0.4) * steps_of(streams_of[2], (NLAT,), ((0, 2),), -0.4, 0.0), -0.4, 0.4),
        "phase_times": jnp.clip(jax.random.uniform(streams_of[3], (SAMPLES,), jnp.float32, -6.0, 6.0) * steps_of(streams_of[3], (SAMPLES,), ((0, 16),), -0.4, 0.0), -6.0, 6.0),
        "phase_weights": jnp.clip(jnp.exp(math.log(0.25) - 3.6888794 * jax.random.uniform(streams_of[4], (SAMPLES,), jnp.float32) ** steps_of(streams_of[4], (SAMPLES,), ((0, 16),), -0.2, 0.2)), 0.00625, 0.25),
    }


radius_scale = 2.5
time_step = 0.5
series_terms = 20


def along_lon(values):
    return (jnp.roll(values, -1, axis=-1) - jnp.roll(values, 1, axis=-1)) * 0.5


def along_lat(values):
    return (values[..., 2:, :] - values[..., :-2, :]) * 0.5


def interior(values):
    return values[..., 1:-1, :]


def wave_operator(fields, coefficients):
    height = fields[:, 0]
    eastward = fields[:, 1]
    northward = fields[:, 2]
    depth_field = coefficients[0]
    rotation = coefficients[1]
    out_height = -(along_lon(interior(depth_field * eastward)) + along_lat(depth_field * northward))
    out_east = -along_lon(interior(height)) + interior(rotation * northward)
    out_north = -along_lat(height) - interior(rotation * eastward)
    return jnp.stack([out_height, out_east, out_north], axis=1) / radius_scale


def advection(fields):
    height = fields[:, 0]
    eastward = fields[:, 1]
    northward = fields[:, 2]
    mid_east = interior(eastward)
    mid_north = interior(northward)
    out_height = -(along_lon(interior(height * eastward)) + along_lat(height * northward))
    out_east = -(mid_east * along_lon(mid_east) + mid_north * along_lat(eastward))
    out_north = -(mid_east * along_lon(mid_north) + mid_north * along_lat(northward))
    return jnp.stack([out_height, out_east, out_north], axis=1)


def series_coeffs(sample_time):
    half_time = sample_time * 0.5
    square = half_time * half_time
    result = []
    for degree in range(DEG + 1):
        summed = jnp.zeros_like(sample_time)
        term_sq = jnp.ones_like(sample_time)
        for series in range(series_terms):
            factor = (-1.0) ** series / (math.factorial(series) * math.factorial(series + degree))
            summed = summed + factor * term_sq
            term_sq = term_sq * square
        result.append(summed * half_time ** degree)
    return result


def pad_rows(values):
    return jnp.pad(values, ((0, 0), (0, 0), (1, 1), (0, 0)))


def exponential(fields, coefficients, sample_time):
    series = series_coeffs(sample_time)
    previous = fields
    accumulated = series[0] * fields
    current = wave_operator(pad_rows(fields), coefficients)
    accumulated = accumulated + 2.0 * series[1] * current
    for degree in range(2, DEG + 1):
        advanced = 2.0 * wave_operator(pad_rows(current), coefficients) + previous
        accumulated = accumulated + 2.0 * series[degree] * advanced
        previous = current
        current = advanced
    return accumulated


def averaged(state_now, coefficients, phase_times, phase_weights):
    def one_sample(summed, paired):
        sample_time, weight = paired
        waves = exponential(state_now[None], coefficients, sample_time)
        pulled = advection(pad_rows(waves))
        returned = exponential(pulled, coefficients, -sample_time)
        return summed + weight * returned[0], None

    summed, unused = lax.scan(one_sample, jnp.zeros_like(state_now), (phase_times, phase_weights))
    return summed


def reference(state_now, ocean_depth, coriolis, phase_times, phase_weights):
    stacked = jnp.stack([ocean_depth, jnp.broadcast_to(coriolis[:, None], ocean_depth.shape)])
    coefficients = jnp.pad(stacked, ((0, 0), (1, 1), (0, 0)))
    first = averaged(state_now, coefficients, phase_times, phase_weights)
    middle = state_now + time_step * first
    second = averaged(middle, coefficients, phase_times, phase_weights)
    tendency = 0.5 * (first + second)
    state_next = state_now + time_step * tendency
    return (state_next, tendency)
```

```python
import functools

import jax
import jax.numpy as jnp
from jax import lax
from jax.experimental import pallas as pl
from jax.experimental.pallas import tpu as pltpu
from jax.sharding import PartitionSpec as P

DEG = 8
TERMS = DEG + 1
LANES = 128
SUBLANES = 8
ROWS_PER_LIMB = 80

radius_scale = 2.5
time_step = 0.5
series_terms = 20

HEIGHT_SCALE = 1.0 / radius_scale
DEPTH_SCALE = 1.0 / (radius_scale * radius_scale)
ROTATION_SCALE = 2.0 / radius_scale


def message_rows(share):
    return -(-(3 * share + 2) // SUBLANES) * SUBLANES


def window_of(tile, width, lane_tiles):
    start = tile * width + width // 2 - LANES // 2 + lane_tiles * LANES
    left = lax.rem(start // LANES, lane_tiles)
    return left, lax.rem(left + 1, lane_tiles), lax.rem(start, LANES)


def split(values):
    high = values.astype(jnp.bfloat16)
    return high, (values - high.astype(jnp.float32)).astype(jnp.bfloat16)


def kernel(
    phases,
    lats,
    nlat,
    state_in,
    depth_in,
    coriolis,
    times,
    weights,
    tend_out,
    state,
    depth,
    message,
    received,
    coef_message,
    coef,
    terms,
    limbs,
    waves,
    pulled,
    sums,
    forward,
    backward,
    out_message,
    out_received,
    input_sem,
    barrier_free_sems,
):
    share, nlon = state.shape[1], state.shape[2]
    rows = depth.shape[0]
    count = phases * lats
    width = nlon // count
    lane_tiles = nlon // LANES
    per_tile = LANES // width
    size = message_rows(share)
    V = nlat // SUBLANES
    group = 80
    phase, lat = lax.axis_index("phase"), lax.axis_index("lat")
    me = lat * phases + phase
    send_sem, recv_sem, coef_send, coef_recv, out_send, out_recv = [barrier_free_sems.at[i] for i in range(6)]

    copies = [
        pltpu.make_async_copy(state_in, state, input_sem.at[0]),
        pltpu.make_async_copy(depth_in, depth, input_sem.at[1]),
    ]
    for copy in copies:
        copy.start()

    unrolled = count <= 32

    def for_steps(start, stop, fn):
        if unrolled:
            for step in range(start, stop):
                fn(step)
        else:

            def body(step, carry):
                fn(step)
                return carry

            lax.fori_loop(start, stop, body, 0)

    def peer_of(step):
        peer = lax.rem(me + step, count)
        return peer, {"phase": lax.rem(peer, phases), "lat": peer // phases}

    barrier = pltpu.get_barrier_semaphore()

    def greet(step):
        pl.semaphore_signal(barrier, inc=1, device_id=peer_of(step)[1])

    for_steps(1, count, greet)

    lane = lax.broadcasted_iota(jnp.int32, (SUBLANES, LANES), 1)
    sub = lax.broadcasted_iota(jnp.int32, (SUBLANES, LANES), 0)
    degree = lane // SUBLANES

    half = jnp.full((SUBLANES, LANES), times[0] * 0.5, jnp.float32)
    weight = jnp.full((SUBLANES, LANES), weights[0], jnp.float32)
    square = half * half
    degree_f = degree.astype(jnp.float32)
    series = jnp.ones_like(half)
    for m in reversed(range(1, series_terms)):
        series = 1.0 - series * square * (1.0 / (m * (degree_f + float(m))))
    power = jnp.ones_like(half)
    scale = jnp.where(degree == 0, 1.0, 0.0)
    for k in range(1, TERMS):
        power = power * (half * (1.0 / k))
        scale = jnp.where(degree == k, 2.0 * power, scale)
    value = series * scale
    flipped = jnp.where(lax.rem(degree, 2) == 0, value, -value)
    coef_rows = jnp.where(sub == 3 * share, flipped, jnp.where(sub == 3 * share + 1, (-0.5 * weight) * value, 0.0))

    copies[0].wait()
    tiles = []
    for t in range(lane_tiles):
        at = slice(t * LANES, (t + 1) * LANES)
        full = coef_rows
        for field in range(3):
            piece = state[field, :, at]
            if field == 0:
                piece = piece * HEIGHT_SCALE
            for r in range(share):
                full = jnp.where(sub == field * share + r, piece[r : r + 1], full)
        tiles.append(full)

    if unrolled:
        for j in range(count):
            start = j * width + width // 2 - LANES // 2 + lane_tiles * LANES
            left = start // LANES % lane_tiles
            value = jnp.where(lane >= start % LANES, tiles[left], tiles[(left + 1) % lane_tiles])
            message[j * size : (j + 1) * size] = value
    else:
        for j in range(count):
            start = j * width + width // 2 - LANES // 2 + lane_tiles * LANES
            left = start // LANES % lane_tiles
            value = jnp.where(lane >= start % LANES, tiles[left], tiles[(left + 1) % lane_tiles])
            message[j * size : (j + 1) * size] = value

    mine = pl.ds(pl.multiple_of(me * size, SUBLANES), size)

    copies[1].wait()
    lane_wide = lax.broadcasted_iota(jnp.int32, (rows, LANES), 1)
    for row in range(rows):
        coef_message[0, rows + row : rows + row + 1] = jnp.full((1, LANES), coriolis[row] * ROTATION_SCALE, jnp.float32)
    for step in range(lats):
        target = lax.rem(lat + step, lats)
        left, right, edge = window_of(target * phases + phase, width, lane_tiles)
        left = depth[:, pl.ds(pl.multiple_of(left * LANES, LANES), LANES)]
        right = depth[:, pl.ds(pl.multiple_of(right * LANES, LANES), LANES)]
        coef_message[step, 0:rows] = jnp.where(lane_wide >= edge, left, right) * DEPTH_SCALE
        if step > 0:
            coef_message[step, rows : 2 * rows] = coef_message[0, rows : 2 * rows]

    own_coef = pl.ds(pl.multiple_of(lat * (2 * rows), SUBLANES), 2 * rows)

    def exchange(step):
        peer, where = peer_of(step)
        return pltpu.make_async_remote_copy(
            src_ref=message.at[pl.ds(pl.multiple_of(peer * size, SUBLANES), size)],
            dst_ref=received.at[mine],
            send_sem=send_sem,
            recv_sem=recv_sem,
            device_id=where,
        )

    def coef_exchange(step):
        return pltpu.make_async_remote_copy(
            src_ref=coef_message.at[step],
            dst_ref=coef.at[own_coef],
            send_sem=coef_send,
            recv_sem=coef_recv,
            device_id={"lat": lax.rem(lat + step, lats)},
        )

    def out_exchange(step):
        peer, where = peer_of(step)
        return pltpu.make_async_remote_copy(
            src_ref=out_message.at[pl.ds(pl.multiple_of(peer * size, SUBLANES), size)],
            dst_ref=out_received.at[mine],
            send_sem=out_send,
            recv_sem=out_recv,
            device_id=where,
        )

    def whole(source, target, length, send, recv):
        return pltpu.make_async_remote_copy(
            src_ref=source.at[pl.ds(0, length)],
            dst_ref=target.at[pl.ds(0, length)],
            send_sem=send,
            recv_sem=recv,
            device_id=peer_of(1)[1],
        )

    all_messages = whole(message, received, (count - 1) * size, send_sem, recv_sem)
    all_outs = whole(out_message, out_received, (count - 1) * size, out_send, out_recv)

    pl.semaphore_wait(barrier, count - 1)
    for step in range(1, lats):
        coef_exchange(step).start()
    for_steps(1, count, lambda step: exchange(step).start())

    received[mine] = message[mine]
    coef[own_coef] = coef_message[0]

    all_messages.wait_recv()
    if lats > 1:
        coef_all = pltpu.make_async_remote_copy(
            src_ref=coef.at[pl.ds(0, (lats - 1) * 2 * rows)],
            dst_ref=coef.at[pl.ds(0, (lats - 1) * 2 * rows)],
            send_sem=coef_send,
            recv_sem=coef_recv,
            device_id=peer_of(1)[1],
        )
        coef_all.wait_recv()

    stride = V // share * size

    def row_slice(field, i):
        return pl.ds(i // share * size + field * share + i % share, SUBLANES, stride)

    start_state = [[received[row_slice(field, i), :] for i in range(V)] for field in range(3)]

    def coef_rows_of(which, i):
        pieces = []
        per = rows // V
        return None

    per = rows // V
    depth_v, rotation_v = [], []
    for i in range(V):
        both = []
        for which in range(2):
            parts = [coef[pl.ds(l * 2 * rows + which * rows + i, per, V), :] for l in range(lats)]
            both.append(jnp.concatenate(parts, axis=0) if lats > 1 else parts[0])
        depth_v.append(both[0])
        rotation_v.append(both[1])

    diagonal = lax.rem(lane, SUBLANES) == sub
    samples = phases
    for s in range(samples):
        at = slice(s * SUBLANES, (s + 1) * SUBLANES)
        row = received[s * size + 3 * share : s * size + 3 * share + 1, :]
        value = jnp.where(diagonal, jnp.broadcast_to(row, (SUBLANES, LANES)), 0.0)
        high = value.astype(jnp.bfloat16).astype(jnp.float32)
        low = value - high
        moved = pltpu.roll(high, group, 1)
        forward[at, 0:LANES] = jnp.where(lane < group, high, moved)
        forward[at, LANES : 2 * LANES] = jnp.where(lane < 2 * group - LANES, moved, pltpu.roll(low, 2 * group - LANES, 1))
        row = received[s * size + 3 * share + 1 : s * size + 3 * share + 2, :]
        backward[at, :] = jnp.where(diagonal, jnp.broadcast_to(row, (SUBLANES, LANES)), 0.0)
    forward_m = forward[...].astype(jnp.bfloat16)[:, : 3 * group]
    back = jnp.transpose(backward[...])[:group]
    back_high, back_low = split(back)
    back_both = jnp.concatenate([back_high, back_high], axis=1)

    def lon_diff(x):
        axis = x.ndim - 1
        return pltpu.roll(x, LANES - 1, axis) - pltpu.roll(x, 1, axis)

    def lat_diffs(xs):
        axis = xs[0].ndim - 2
        place = lax.broadcasted_iota(jnp.int32, xs[0].shape, axis)
        before = jnp.where(place == 0, 0.0, pltpu.roll(xs[-1], 1, axis))
        after = jnp.where(place == SUBLANES - 1, 0.0, pltpu.roll(xs[0], SUBLANES - 1, axis))
        return [(xs[i + 1] if i < V - 1 else after) - (xs[i - 1] if i > 0 else before) for i in range(V)]

    def applied(height, east, north):
        flux = lat_diffs([depth_v[i] * north[i] for i in range(V)])
        slope = lat_diffs(height)
        out = [[], [], []]
        for i in range(V):
            out[0].append(lon_diff(depth_v[i] * east[i]) + flux[i])
            out[1].append(lon_diff(height[i]) - rotation_v[i] * north[i])
            out[2].append(slope[i] + rotation_v[i] * east[i])
        return out

    def lane_tile(i):
        return slice(i * LANES, (i + 1) * LANES)

    def averaged(fields):
        previous = fields
        current = [[0.5 * x for x in field] for field in applied(*fields)]

        def store(k, values):
            for field in range(3):
                for i in range(V):
                    terms[field, k * SUBLANES : (k + 1) * SUBLANES, lane_tile(i)] = values[field][i]

        store(0, previous)
        store(1, current)
        for k in range(2, TERMS):
            step = applied(*current)
            previous, current = current, [[step[f][i] + previous[f][i] for i in range(V)] for f in range(3)]
            store(k, current)
        for field in range(3):
            high, low = split(terms[field])
            limbs[field, 0:group] = high
            limbs[field, group : 2 * group] = low
            limbs[field, 2 * group : 3 * group] = high
        for field in range(3):
            waves[field] = jnp.dot(forward_m, limbs[field], preferred_element_type=jnp.float32)

        pair = 2 * SUBLANES
        half_rows = samples * SUBLANES

        def advect(j, carry):
            at = pl.multiple_of(j * pair, pair)
            got = [
                [waves[f, pl.ds(at, pair), lane_tile(i)].reshape(2, SUBLANES, LANES) for i in range(V)] for f in range(3)
            ]
            height, east, north = got
            flux = lat_diffs([height[i] * north[i] for i in range(V)])
            east_lat, north_lat = lat_diffs(east), lat_diffs(north)
            for i in range(V):
                values = (
                    lon_diff(height[i] * east[i]) + flux[i],
                    east[i] * lon_diff(east[i]) + north[i] * east_lat[i],
                    east[i] * lon_diff(north[i]) + north[i] * north_lat[i],
                )
                for f in range(3):
                    high, low = split(values[f].reshape(pair, LANES))
                    pulled[f, pl.ds(at, pair), lane_tile(i)] = high
                    pulled[f, pl.ds(pl.multiple_of(half_rows + at, pair), pair), lane_tile(i)] = low
            return carry

        lax.fori_loop(0, samples // 2, advect, 0)

        for field in range(3):
            sums[field] = jnp.dot(back_both, pulled[field], preferred_element_type=jnp.float32) + jnp.dot(
                back_low, pulled[field, 0:half_rows], preferred_element_type=jnp.float32
            )

        def term(k):
            return [[sums[f, k * SUBLANES : (k + 1) * SUBLANES, lane_tile(i)] for i in range(V)] for f in range(3)]

        after, now = None, term(DEG)
        for k in reversed(range(1, DEG)):
            step, own = applied(*now), term(k)
            following = [
                [own[f][i] + step[f][i] + (after[f][i] if after is not None else 0.0) for i in range(V)] for f in range(3)
            ]
            after, now = now, following
        step, own = applied(*now), term(0)
        return [[own[f][i] + after[f][i] + 0.5 * step[f][i] for i in range(V)] for f in range(3)]

    terms[:, TERMS * SUBLANES :] = jnp.zeros((3, group - TERMS * SUBLANES, V * LANES), jnp.float32)
    first = averaged(start_state)
    middle = [[start_state[f][i] + time_step * first[f][i] for i in range(V)] for f in range(3)]
    second = averaged(middle)

    for field in range(3):
        factor = 0.5 * radius_scale if field == 0 else 0.5
        for i in range(V):
            out_message[row_slice(field, i), :] = factor * (first[field][i] + second[field][i])

    for_steps(1, count, lambda step: out_exchange(step).start())
    out_received[mine] = out_message[mine]
    all_outs.wait_recv()

    for t in range(lane_tiles):
        total = out_received[t * per_tile * size : (t * per_tile + 1) * size]
        for j in range(1, per_tile):
            at = (t * per_tile + j) * size
            total = jnp.where(lane >= j * width, out_received[at : at + size], total)
        for field in range(3):
            tend_out[field, :, lane_tile(t)] = total[field * share : (field + 1) * share]

    all_messages.wait_send()
    all_outs.wait_send()
    if lats > 1:
        coef_all.wait_send()


def finish(state, tendency, next_out, tend_out):
    tend_out[...] = tendency[...]
    next_out[...] = state[...] + time_step * tendency[...]


def per_device(phases, lats, nlat, state_now, ocean_depth, coriolis, phase_times, phase_weights):
    rows, share = ocean_depth.shape[0], state_now.shape[1]
    nlon = ocean_depth.shape[1]
    count = phases * lats
    size = message_rows(share)
    wide = nlat // SUBLANES * LANES
    samples = phases
    group = 80
    vmem = pl.BlockSpec(memory_space=pltpu.VMEM)
    smem = pl.BlockSpec(memory_space=pltpu.SMEM)
    any_space = pl.BlockSpec(memory_space=pl.ANY)
    out = jax.ShapeDtypeStruct(state_now.shape, jnp.float32)
    f32, bf16 = jnp.float32, jnp.bfloat16
    scratch = [
        pltpu.VMEM(state_now.shape, f32),
        pltpu.VMEM(ocean_depth.shape, f32),
        pltpu.VMEM((count * size, LANES), f32),
        pltpu.VMEM((count * size, LANES), f32),
        pltpu.VMEM((lats, 2 * rows, LANES), f32),
        pltpu.VMEM((lats * 2 * rows, LANES), f32),
        pltpu.VMEM((3, group, wide), f32),
        pltpu.VMEM((3, 3 * group, wide), bf16),
        pltpu.VMEM((3, samples * SUBLANES, wide), f32),
        pltpu.VMEM((3, 2 * samples * SUBLANES, wide), bf16),
        pltpu.VMEM((3, group, wide), f32),
        pltpu.VMEM((samples * SUBLANES, 2 * LANES), f32),
        pltpu.VMEM((samples * SUBLANES, LANES), f32),
        pltpu.VMEM((count * size, LANES), f32),
        pltpu.VMEM((count * size, LANES), f32),
        pltpu.SemaphoreType.DMA((2,)),
        pltpu.SemaphoreType.DMA((6,)),
    ]
    tendency = pl.pallas_call(
        functools.partial(kernel, phases, lats, nlat),
        out_shape=out,
        in_specs=[any_space, any_space, smem, smem, smem],
        out_specs=vmem,
        scratch_shapes=scratch,
        compiler_params=pltpu.CompilerParams(
            collective_id=0, has_side_effects=True, vmem_limit_bytes=(56 if wide > 1024 else 32) * 1024 * 1024
        ),
    )(state_now, ocean_depth, coriolis, phase_times, phase_weights)
    return pl.pallas_call(
        finish,
        out_shape=(out, out),
        in_specs=[vmem, vmem],
        out_specs=(vmem, vmem),
    )(state_now, tendency)


def solution(mesh):
    placed = (P(None, ("lat", "phase"), None), P("lat", None), P("lat"), P("phase"), P("phase"))

    def step(state_now, ocean_depth, coriolis, phase_times, phase_weights):
        return jax.shard_map(
            functools.partial(per_device, mesh.shape["phase"], mesh.shape["lat"], state_now.shape[1]),
            mesh=mesh,
            in_specs=placed,
            out_specs=(P(None, ("lat", "phase"), None), P(None, ("lat", "phase"), None)),
            check_vma=False,
        )(state_now, ocean_depth, coriolis, phase_times, phase_weights)

    return step
```

```python
import functools

import jax
import jax.numpy as jnp
from jax import lax
from jax.experimental import pallas as pl
from jax.experimental.pallas import tpu as pltpu
from jax.sharding import PartitionSpec as P

DEG = 8
TERMS = DEG + 1
LANES = 128
SUBLANES = 8
ROWS_PER_LIMB = 80

radius_scale = 2.5
time_step = 0.5
series_terms = 20

HEIGHT_SCALE = 1.0 / radius_scale
DEPTH_SCALE = 1.0 / (radius_scale * radius_scale)
ROTATION_SCALE = 2.0 / radius_scale


def message_rows(share):
    return -(-(3 * share + 2) // SUBLANES) * SUBLANES


HALO = 4 * DEG + 2


def tiles_of(phases, lats, nlon):
    computing = min(phases, -(-nlon // ((LANES - 2 * HALO) * lats)))
    return computing, computing * lats


def window_of(tile, tiles, nlon):
    start = tile * nlon // tiles - HALO + nlon
    left = start // LANES % (nlon // LANES)
    return left, (left + 1) % (nlon // LANES), start % LANES


def split(values):
    high = values.astype(jnp.bfloat16)
    return high, (values - high.astype(jnp.float32)).astype(jnp.bfloat16)


def kernel(
    phases,
    lats,
    nlat,
    state_in,
    depth_in,
    coriolis_in,
    times,
    weights,
    next_out,
    tend_out,
    state,
    depth,
    coriolis,
    message,
    received,
    coef_message,
    coef,
    terms,
    limbs,
    waves,
    pulled,
    sums,
    forward,
    backward,
    out_message,
    out_received,
    input_sem,
    barrier_free_sems,
):
    share, nlon = state.shape[1], state.shape[2]
    rows = depth.shape[0]
    count = phases * lats
    computing, tiles = tiles_of(phases, lats, nlon)
    lane_tiles = nlon // LANES
    size = message_rows(share)
    V = nlat // SUBLANES
    group = 80
    phase, lat = lax.axis_index("phase"), lax.axis_index("lat")
    me = lat * phases + phase
    mine_tile = phase * lats + lat
    computes = phase < computing
    send_sem, recv_sem, coef_send, coef_recv, out_send, out_recv = [barrier_free_sems.at[i] for i in range(6)]

    unrolled = count <= 32

    def for_steps(start, stop, fn):
        if unrolled:
            for step in range(start, stop):
                fn(step)
        else:

            def body(step, carry):
                fn(step)
                return carry

            lax.fori_loop(start, stop, body, 0)

    def device(tile):
        return {"phase": tile // lats, "lat": tile % lats}

    def for_others(stop, fn):
        def one(tile):
            pl.when(mine_tile != tile)(lambda: fn(tile))

        for_steps(0, stop, one)

    barrier = pltpu.get_barrier_semaphore()

    @pl.when(computes)
    def _():
        for_others(count, lambda tile: pl.semaphore_signal(barrier, inc=1, device_id=device(tile)))

    pairs = ((state_in, state), (coriolis_in, coriolis), (depth_in, depth))
    copies = [pltpu.make_async_copy(source, target, input_sem.at[i]) for i, (source, target) in enumerate(pairs)]
    copies[0].start()

    @pl.when(computes)
    def _():
        copies[1].start()
        copies[2].start()

    lane = lax.broadcasted_iota(jnp.int32, (SUBLANES, LANES), 1)
    sub = lax.broadcasted_iota(jnp.int32, (SUBLANES, LANES), 0)
    degree = lane // SUBLANES

    half = jnp.full((SUBLANES, LANES), times[0] * 0.5, jnp.float32)
    weight = jnp.full((SUBLANES, LANES), weights[0], jnp.float32)
    square = half * half
    degree_f = degree.astype(jnp.float32)
    series = jnp.ones_like(half)
    for m in reversed(range(1, series_terms)):
        series = 1.0 - series * square * (1.0 / (m * (degree_f + float(m))))
    power = jnp.ones_like(half)
    scale = jnp.where(degree == 0, 1.0, 0.0)
    for k in range(1, TERMS):
        power = power * (half * (1.0 / k))
        scale = jnp.where(degree == k, 2.0 * power, scale)
    value = series * scale
    flipped = jnp.where(lax.rem(degree, 2) == 0, value, -value)
    coef_rows = jnp.where(sub == 3 * share, flipped, jnp.where(sub == 3 * share + 1, (-0.5 * weight) * value, 0.0))

    copies[0].wait()
    pieces = []
    for t in range(lane_tiles):
        at = slice(t * LANES, (t + 1) * LANES)
        full = coef_rows
        for field in range(3):
            piece = state[field, :, at]
            if field == 0:
                piece = piece * HEIGHT_SCALE
            for r in range(share):
                full = jnp.where(sub == field * share + r, piece[r : r + 1], full)
        pieces.append(full)

    for tile in range(tiles):
        left, right, edge = window_of(tile, tiles, nlon)
        message[tile * size : (tile + 1) * size] = jnp.where(lane >= edge, pieces[left], pieces[right])

    mine = pl.ds(pl.multiple_of(me * size, SUBLANES), size)

    own_coef = pl.ds(pl.multiple_of(lat * (2 * rows), SUBLANES), 2 * rows)

    def exchange(tile):
        return pltpu.make_async_remote_copy(
            src_ref=message.at[pl.ds(tile * size, size)],
            dst_ref=received.at[mine],
            send_sem=send_sem,
            recv_sem=recv_sem,
            device_id=device(tile),
        )

    def coef_exchange(step):
        return pltpu.make_async_remote_copy(
            src_ref=coef_message.at[step],
            dst_ref=coef.at[own_coef],
            send_sem=coef_send,
            recv_sem=coef_recv,
            device_id={"lat": lax.rem(lat + step, lats)},
        )

    def owner_rows(tile):
        return pl.ds(pl.multiple_of((tile % lats * phases + tile // lats) * size, SUBLANES), size)

    def out_exchange(tile):
        return pltpu.make_async_remote_copy(
            src_ref=out_message.at[owner_rows(tile)],
            dst_ref=out_received.at[pl.ds(pl.multiple_of(mine_tile * size, SUBLANES), size)],
            send_sem=out_send,
            recv_sem=out_recv,
            device_id=device(tile),
        )

    def all_of(array, number, length, send, recv):
        part = array.at[pl.ds(0, number * length)]
        return pltpu.make_async_remote_copy(
            src_ref=part, dst_ref=part, send_sem=send, recv_sem=recv, device_id=device(0)
        )

    def compute():
        received[mine] = message[pl.ds(pl.multiple_of(mine_tile * size, SUBLANES), size)]
        copies[1].wait()
        copies[2].wait()
        lane_wide = lax.broadcasted_iota(jnp.int32, (rows, LANES), 1)
        for row in range(rows):
            coef_message[0, rows + row : rows + row + 1] = jnp.full((1, LANES), coriolis[row] * ROTATION_SCALE, jnp.float32)
        for step in range(lats):
            target = lax.rem(lat + step, lats)
            left, right, edge = window_of(phase * lats + target, tiles, nlon)
            left = depth[:, pl.ds(pl.multiple_of(left * LANES, LANES), LANES)]
            right = depth[:, pl.ds(pl.multiple_of(right * LANES, LANES), LANES)]
            coef_message[step, 0:rows] = jnp.where(lane_wide >= edge, left, right) * DEPTH_SCALE
            if step > 0:
                coef_message[step, rows : 2 * rows] = coef_message[0, rows : 2 * rows]

        for step in range(1, lats):
            coef_exchange(step).start()
        coef[own_coef] = coef_message[0]

        all_of(received, count - 1, size, send_sem, recv_sem).wait_recv()
        if lats > 1:
            coef_all = all_of(coef, lats - 1, 2 * rows, coef_send, coef_recv)
            coef_all.wait_recv()

        stride = V // share * size

        def row_slice(field, i):
            return pl.ds(i // share * size + field * share + i % share, SUBLANES, stride)

        start_state = [[received[row_slice(field, i), :] for i in range(V)] for field in range(3)]

        per = rows // V
        depth_v, rotation_v = [], []
        for i in range(V):
            both = []
            for which in range(2):
                parts = [coef[pl.ds(l * 2 * rows + which * rows + i, per, V), :] for l in range(lats)]
                both.append(jnp.concatenate(parts, axis=0) if lats > 1 else parts[0])
            depth_v.append(both[0])
            rotation_v.append(both[1])

        diagonal = lax.rem(lane, SUBLANES) == sub
        samples = phases
        for s in range(samples):
            at = slice(s * SUBLANES, (s + 1) * SUBLANES)
            row = received[s * size + 3 * share : s * size + 3 * share + 1, :]
            value = jnp.where(diagonal, jnp.broadcast_to(row, (SUBLANES, LANES)), 0.0)
            high = value.astype(jnp.bfloat16).astype(jnp.float32)
            low = value - high
            moved = pltpu.roll(high, group, 1)
            forward[at, 0:LANES] = jnp.where(lane < group, high, moved)
            forward[at, LANES : 2 * LANES] = jnp.where(lane < 2 * group - LANES, moved, pltpu.roll(low, 2 * group - LANES, 1))
            row = received[s * size + 3 * share + 1 : s * size + 3 * share + 2, :]
            backward[at, :] = jnp.where(diagonal, jnp.broadcast_to(row, (SUBLANES, LANES)), 0.0)
        forward_m = forward[...].astype(jnp.bfloat16)[:, : 3 * group]
        back = jnp.transpose(backward[...])[:group]
        back_high, back_low = split(back)
        back_both = jnp.concatenate([back_high, back_high], axis=1)

        def lon_diff(x):
            axis = x.ndim - 1
            return pltpu.roll(x, LANES - 1, axis) - pltpu.roll(x, 1, axis)

        def lat_diffs(xs):
            axis = xs[0].ndim - 2
            place = lax.broadcasted_iota(jnp.int32, xs[0].shape, axis)
            before = jnp.where(place == 0, 0.0, pltpu.roll(xs[-1], 1, axis))
            after = jnp.where(place == SUBLANES - 1, 0.0, pltpu.roll(xs[0], SUBLANES - 1, axis))
            return [(xs[i + 1] if i < V - 1 else after) - (xs[i - 1] if i > 0 else before) for i in range(V)]

        def applied(height, east, north):
            flux = lat_diffs([depth_v[i] * north[i] for i in range(V)])
            slope = lat_diffs(height)
            out = [[], [], []]
            for i in range(V):
                out[0].append(lon_diff(depth_v[i] * east[i]) + flux[i])
                out[1].append(lon_diff(height[i]) - rotation_v[i] * north[i])
                out[2].append(slope[i] + rotation_v[i] * east[i])
            return out

        def lane_tile(i):
            return slice(i * LANES, (i + 1) * LANES)

        def averaged(fields):
            previous = fields
            current = [[0.5 * x for x in field] for field in applied(*fields)]

            def store(k, values):
                for field in range(3):
                    for i in range(V):
                        terms[field, k * SUBLANES : (k + 1) * SUBLANES, lane_tile(i)] = values[field][i]

            store(0, previous)
            store(1, current)
            for k in range(2, TERMS):
                step = applied(*current)
                previous, current = current, [[step[f][i] + previous[f][i] for i in range(V)] for f in range(3)]
                store(k, current)
            for field in range(3):
                high, low = split(terms[field])
                limbs[field, 0:group] = high
                limbs[field, group : 2 * group] = low
                limbs[field, 2 * group : 3 * group] = high
            for field in range(3):
                waves[field] = jnp.dot(forward_m, limbs[field], preferred_element_type=jnp.float32)

            pair = 2 * SUBLANES
            half_rows = samples * SUBLANES

            def advect(j, carry):
                at = pl.multiple_of(j * pair, pair)
                got = [
                    [waves[f, pl.ds(at, pair), lane_tile(i)].reshape(2, SUBLANES, LANES) for i in range(V)] for f in range(3)
                ]
                height, east, north = got
                flux = lat_diffs([height[i] * north[i] for i in range(V)])
                east_lat, north_lat = lat_diffs(east), lat_diffs(north)
                for i in range(V):
                    values = (
                        lon_diff(height[i] * east[i]) + flux[i],
                        east[i] * lon_diff(east[i]) + north[i] * east_lat[i],
                        east[i] * lon_diff(north[i]) + north[i] * north_lat[i],
                    )
                    for f in range(3):
                        high, low = split(values[f].reshape(pair, LANES))
                        pulled[f, pl.ds(at, pair), lane_tile(i)] = high
                        pulled[f, pl.ds(pl.multiple_of(half_rows + at, pair), pair), lane_tile(i)] = low
                return carry

            lax.fori_loop(0, samples // 2, advect, 0)

            for field in range(3):
                sums[field] = jnp.dot(back_both, pulled[field], preferred_element_type=jnp.float32) + jnp.dot(
                    back_low, pulled[field, 0:half_rows], preferred_element_type=jnp.float32
                )

            def term(k):
                return [[sums[f, k * SUBLANES : (k + 1) * SUBLANES, lane_tile(i)] for i in range(V)] for f in range(3)]

            after, now = None, term(DEG)
            for k in reversed(range(1, DEG)):
                step, own = applied(*now), term(k)
                following = [
                    [own[f][i] + step[f][i] + (after[f][i] if after is not None else 0.0) for i in range(V)] for f in range(3)
                ]
                after, now = now, following
            step, own = applied(*now), term(0)
            return [[own[f][i] + after[f][i] + 0.5 * step[f][i] for i in range(V)] for f in range(3)]

        terms[:, TERMS * SUBLANES :] = jnp.zeros((3, group - TERMS * SUBLANES, V * LANES), jnp.float32)
        first = averaged(start_state)
        middle = [[start_state[f][i] + time_step * first[f][i] for i in range(V)] for f in range(3)]
        second = averaged(middle)

        for field in range(3):
            factor = 0.5 * radius_scale if field == 0 else 0.5
            for i in range(V):
                out_message[row_slice(field, i), :] = factor * (first[field][i] + second[field][i])

        for_others(count, lambda tile: out_exchange(tile).start())
        mine_out = pl.ds(pl.multiple_of(mine_tile * size, SUBLANES), size)
        out_received[mine_out] = out_message[mine]
        if lats > 1:
            coef_all.wait_send()

    pl.semaphore_wait(barrier, tiles - computes.astype(jnp.int32))
    for_others(tiles, lambda tile: exchange(tile).start())

    @pl.when(computes)
    def _():
        compute()
        all_of(message, tiles - 1, size, send_sem, recv_sem).wait_send()
        all_of(out_received, tiles - 1, size, out_send, out_recv).wait_recv()

    @pl.when(jnp.logical_not(computes))
    def _():
        all_of(message, tiles, size, send_sem, recv_sem).wait_send()
        all_of(out_received, tiles, size, out_send, out_recv).wait_recv()

    starts = [tile * nlon // tiles for tile in range(tiles)] + [nlon]
    for t in range(lane_tiles):
        total = None
        for tile in range(tiles):
            if starts[tile] < (t + 1) * LANES and starts[tile + 1] > t * LANES:
                got = out_received[tile * size : (tile + 1) * size]
                total = got if total is None else jnp.where(lane >= starts[tile] - t * LANES, got, total)
        for field in range(3):
            at = slice(t * LANES, (t + 1) * LANES)
            piece = total[field * share : (field + 1) * share]
            tend_out[field, :, at] = piece
            next_out[field, :, at] = state[field, :, at] + time_step * piece

    @pl.when(computes)
    def _():
        all_of(out_message, count - 1, size, out_send, out_recv).wait_send()


def per_device(phases, lats, nlat, state_now, ocean_depth, coriolis, phase_times, phase_weights):
    rows, share = ocean_depth.shape[0], state_now.shape[1]
    nlon = ocean_depth.shape[1]
    count = phases * lats
    size = message_rows(share)
    tiles = tiles_of(phases, lats, nlon)[1]
    wide = nlat // SUBLANES * LANES
    samples = phases
    group = 80
    vmem = pl.BlockSpec(memory_space=pltpu.VMEM)
    hbm = pl.BlockSpec(memory_space=pltpu.HBM)
    smem = pl.BlockSpec(memory_space=pltpu.SMEM)
    out = jax.ShapeDtypeStruct(state_now.shape, jnp.float32)
    f32, bf16 = jnp.float32, jnp.bfloat16
    scratch = [
        pltpu.VMEM(state_now.shape, f32),
        pltpu.VMEM(ocean_depth.shape, f32),
        pltpu.SMEM(coriolis.shape, f32),
        pltpu.VMEM((tiles * size, LANES), f32),
        pltpu.VMEM((count * size, LANES), f32),
        pltpu.VMEM((lats, 2 * rows, LANES), f32),
        pltpu.VMEM((lats * 2 * rows, LANES), f32),
        pltpu.VMEM((3, group, wide), f32),
        pltpu.VMEM((3, 3 * group, wide), bf16),
        pltpu.VMEM((3, samples * SUBLANES, wide), f32),
        pltpu.VMEM((3, 2 * samples * SUBLANES, wide), bf16),
        pltpu.VMEM((3, group, wide), f32),
        pltpu.VMEM((samples * SUBLANES, 2 * LANES), f32),
        pltpu.VMEM((samples * SUBLANES, LANES), f32),
        pltpu.VMEM((count * size, LANES), f32),
        pltpu.VMEM((tiles * size, LANES), f32),
        pltpu.SemaphoreType.DMA((3,)),
        pltpu.SemaphoreType.DMA((6,)),
    ]
    return pl.pallas_call(
        functools.partial(kernel, phases, lats, nlat),
        out_shape=(out, out),
        in_specs=[hbm, hbm, hbm, smem, smem],
        out_specs=(vmem, vmem),
        scratch_shapes=scratch,
        compiler_params=pltpu.CompilerParams(
            collective_id=0, has_side_effects=True, vmem_limit_bytes=(56 if wide > 1024 else 32) * 1024 * 1024
        ),
    )(*[pltpu.with_memory_space_constraint(a, pltpu.HBM) for a in (state_now, ocean_depth, coriolis)], phase_times, phase_weights)


def solution(mesh):
    placed = (P(None, ("lat", "phase"), None), P("lat", None), P("lat"), P("phase"), P("phase"))

    def step(state_now, ocean_depth, coriolis, phase_times, phase_weights):
        return jax.shard_map(
            functools.partial(per_device, mesh.shape["phase"], mesh.shape["lat"], state_now.shape[1]),
            mesh=mesh,
            in_specs=placed,
            out_specs=(P(None, ("lat", "phase"), None), P(None, ("lat", "phase"), None)),
            check_vma=False,
        )(state_now, ocean_depth, coriolis, phase_times, phase_weights)

    return step
```

```python
import functools

import jax
import jax.numpy as jnp
from jax import lax
from jax.experimental import pallas as pl
from jax.experimental.pallas import tpu as pltpu
from jax.sharding import PartitionSpec as P

DEG = 8
TERMS = DEG + 1
LANES = 128
SUBLANES = 8
ROWS_PER_LIMB = 80

radius_scale = 2.5
time_step = 0.5
series_terms = 20

HEIGHT_SCALE = 1.0 / radius_scale
DEPTH_SCALE = 1.0 / (radius_scale * radius_scale)
ROTATION_SCALE = 2.0 / radius_scale


def message_rows(share):
    return -(-(3 * share + 2) // SUBLANES) * SUBLANES


HALO = 4 * DEG + 2


def tiles_of(phases, lats, nlon):
    computing = min(phases, -(-nlon // ((LANES - 2 * HALO) * lats)))
    return computing, computing * lats


def window_of(tile, tiles, nlon):
    start = tile * nlon // tiles - HALO + nlon
    left = start // LANES % (nlon // LANES)
    return left, (left + 1) % (nlon // LANES), start % LANES


def split(values):
    high = values.astype(jnp.bfloat16)
    return high, (values - high.astype(jnp.float32)).astype(jnp.bfloat16)


def kernel(
    phases,
    lats,
    nlat,
    state_in,
    depth_in,
    coriolis_in,
    times,
    weights,
    next_out,
    tend_out,
    state,
    depth,
    coriolis,
    message,
    received,
    coef_message,
    coef,
    limbs,
    waves,
    pulled,
    sums,
    series_rows,
    out_message,
    out_received,
    input_sem,
    barrier_free_sems,
):
    share, nlon = state.shape[1], state.shape[2]
    rows = depth.shape[0]
    count = phases * lats
    computing, tiles = tiles_of(phases, lats, nlon)
    lane_tiles = nlon // LANES
    size = message_rows(share)
    V = nlat // SUBLANES
    group = 80
    phase, lat = lax.axis_index("phase"), lax.axis_index("lat")
    me = lat * phases + phase
    mine_tile = phase * lats + lat
    computes = phase < computing
    send_sem, recv_sem, coef_send, coef_recv, out_send, out_recv = [barrier_free_sems.at[i] for i in range(6)]

    unrolled = count <= 32

    def for_steps(start, stop, fn):
        if unrolled:
            for step in range(start, stop):
                fn(step)
        else:

            def body(step, carry):
                fn(step)
                return carry

            lax.fori_loop(start, stop, body, 0)

    def device(tile):
        return {"phase": tile // lats, "lat": tile % lats}

    def for_others(stop, fn):
        def one(tile):
            pl.when(mine_tile != tile)(lambda: fn(tile))

        for_steps(0, stop, one)

    def for_tiles_back(fn):
        def one(back):
            tile = tiles - 1 - back
            pl.when(mine_tile != tile)(lambda: fn(tile))

        for_steps(0, tiles, one)

    barrier = pltpu.get_barrier_semaphore()

    @pl.when(computes)
    def _():
        for_others(count, lambda tile: pl.semaphore_signal(barrier, inc=1, device_id=device(tile)))

    pairs = ((state_in, state), (coriolis_in, coriolis), (depth_in, depth))
    copies = [pltpu.make_async_copy(source, target, input_sem.at[i]) for i, (source, target) in enumerate(pairs)]
    copies[0].start()

    @pl.when(computes)
    def _():
        copies[1].start()
        copies[2].start()

    lane = lax.broadcasted_iota(jnp.int32, (SUBLANES, LANES), 1)
    sub = lax.broadcasted_iota(jnp.int32, (SUBLANES, LANES), 0)
    degree = lane // SUBLANES

    half = jnp.full((SUBLANES, LANES), times[0] * 0.5, jnp.float32)
    weight = jnp.full((SUBLANES, LANES), weights[0], jnp.float32)
    square = half * half
    degree_f = degree.astype(jnp.float32)
    series = jnp.ones_like(half)
    for m in reversed(range(1, series_terms)):
        series = 1.0 - series * square * (1.0 / (m * (degree_f + float(m))))
    power = jnp.ones_like(half)
    scale = jnp.where(degree == 0, 1.0, 0.0)
    for k in range(1, TERMS):
        power = power * (half * (1.0 / k))
        scale = jnp.where(degree == k, 2.0 * power, scale)
    value = series * scale
    flipped = jnp.where(lax.rem(degree, 2) == 0, value, -value)
    coef_rows = jnp.where(sub == 3 * share, flipped, jnp.where(sub == 3 * share + 1, (-0.5 * weight) * value, 0.0))

    copies[0].wait()
    pieces = []
    for t in range(lane_tiles):
        at = slice(t * LANES, (t + 1) * LANES)
        full = coef_rows
        for field in range(3):
            piece = state[field, :, at]
            if field == 0:
                piece = piece * HEIGHT_SCALE
            for r in range(share):
                full = jnp.where(sub == field * share + r, piece[r : r + 1], full)
        pieces.append(full)

    for tile in range(tiles):
        left, right, edge = window_of(tile, tiles, nlon)
        message[tile * size : (tile + 1) * size] = jnp.where(lane >= edge, pieces[left], pieces[right])

    mine = pl.ds(pl.multiple_of(me * size, SUBLANES), size)

    own_coef = pl.ds(pl.multiple_of(lat * (2 * rows), SUBLANES), 2 * rows)

    def exchange(tile):
        return pltpu.make_async_remote_copy(
            src_ref=message.at[pl.ds(tile * size, size)],
            dst_ref=received.at[mine],
            send_sem=send_sem,
            recv_sem=recv_sem,
            device_id=device(tile),
        )

    def coef_exchange(step):
        return pltpu.make_async_remote_copy(
            src_ref=coef_message.at[step],
            dst_ref=coef.at[own_coef],
            send_sem=coef_send,
            recv_sem=coef_recv,
            device_id={"lat": lax.rem(lat + step, lats)},
        )

    def owner_rows(tile):
        return pl.ds(pl.multiple_of((tile % lats * phases + tile // lats) * size, SUBLANES), size)

    def out_exchange(tile):
        return pltpu.make_async_remote_copy(
            src_ref=out_message.at[owner_rows(tile)],
            dst_ref=out_received.at[pl.ds(pl.multiple_of(mine_tile * size, SUBLANES), size)],
            send_sem=out_send,
            recv_sem=out_recv,
            device_id=device(tile),
        )

    def all_of(array, number, length, send, recv):
        part = array.at[pl.ds(0, number * length)]
        return pltpu.make_async_remote_copy(
            src_ref=part, dst_ref=part, send_sem=send, recv_sem=recv, device_id=device(0)
        )

    def compute():
        received[mine] = message[pl.ds(pl.multiple_of(mine_tile * size, SUBLANES), size)]
        copies[1].wait()
        copies[2].wait()
        lane_wide = lax.broadcasted_iota(jnp.int32, (rows, LANES), 1)
        for row in range(rows):
            coef_message[0, rows + row : rows + row + 1] = jnp.full((1, LANES), coriolis[row] * ROTATION_SCALE, jnp.float32)
        for step in range(lats):
            target = lax.rem(lat + step, lats)
            left, right, edge = window_of(phase * lats + target, tiles, nlon)
            left = depth[:, pl.ds(pl.multiple_of(left * LANES, LANES), LANES)]
            right = depth[:, pl.ds(pl.multiple_of(right * LANES, LANES), LANES)]
            coef_message[step, 0:rows] = jnp.where(lane_wide >= edge, left, right) * DEPTH_SCALE
            if step > 0:
                coef_message[step, rows : 2 * rows] = coef_message[0, rows : 2 * rows]

        for step in range(1, lats):
            coef_exchange(step).start()
        coef[own_coef] = coef_message[0]

        if lats > 1:
            coef_all = all_of(coef, lats - 1, 2 * rows, coef_send, coef_recv)
            coef_all.wait_recv()

        stride = V // share * size

        def row_slice(field, i):
            return pl.ds(i // share * size + field * share + i % share, SUBLANES, stride)

        per = rows // V
        depth_v, rotation_v = [], []
        for i in range(V):
            both = []
            for which in range(2):
                parts = [coef[pl.ds(l * 2 * rows + which * rows + i, per, V), :] for l in range(lats)]
                both.append(jnp.concatenate(parts, axis=0) if lats > 1 else parts[0])
            depth_v.append(both[0])
            rotation_v.append(both[1])

        all_of(received, count - 1, size, send_sem, recv_sem).wait_recv()
        start_state = [[received[row_slice(field, i), :] for i in range(V)] for field in range(3)]

        diagonal = lax.rem(lane, SUBLANES) == sub
        samples = phases
        lane_s = lax.broadcasted_iota(jnp.int32, (samples, LANES), 1)
        value = received[pl.ds(3 * share, samples, size), :]
        high = value.astype(jnp.bfloat16).astype(jnp.float32)
        moved = pltpu.roll(high, group, 1)
        series_rows[0] = jnp.where(lane_s < group, high, moved)
        low = pltpu.roll(value - high, 2 * group - LANES, 1)
        series_rows[1] = jnp.where(lane_s < 2 * group - LANES, moved, low)
        series_rows[2] = received[pl.ds(3 * share + 1, samples, size), :]

        def spread(which):
            rows_of = [jnp.broadcast_to(series_rows[which, s : s + 1, :], (SUBLANES, LANES)) for s in range(samples)]
            return jnp.concatenate([jnp.where(diagonal, row, 0.0) for row in rows_of])

        forward_m = jnp.concatenate([spread(0).astype(jnp.bfloat16), spread(1).astype(jnp.bfloat16)], axis=1)[:, : 3 * group]
        back = jnp.transpose(spread(2))[:group]
        back_high, back_low = split(back)
        back_both = jnp.concatenate(
            [jnp.concatenate([back_high, back_high], axis=1), jnp.concatenate([back_low, jnp.zeros_like(back_low)], axis=1)]
        )

        def lon_diff(x):
            axis = x.ndim - 1
            return pltpu.roll(x, LANES - 1, axis) - pltpu.roll(x, 1, axis)

        def lat_diffs(xs):
            axis = xs[0].ndim - 2
            place = lax.broadcasted_iota(jnp.int32, xs[0].shape, axis)
            before = jnp.where(place == 0, 0.0, pltpu.roll(xs[-1], 1, axis))
            after = jnp.where(place == SUBLANES - 1, 0.0, pltpu.roll(xs[0], SUBLANES - 1, axis))
            return [(xs[i + 1] if i < V - 1 else after) - (xs[i - 1] if i > 0 else before) for i in range(V)]

        def applied(height, east, north):
            flux = lat_diffs([depth_v[i] * north[i] for i in range(V)])
            slope = lat_diffs(height)
            out = [[], [], []]
            for i in range(V):
                out[0].append(lon_diff(depth_v[i] * east[i]) + flux[i])
                out[1].append(lon_diff(height[i]) - rotation_v[i] * north[i])
                out[2].append(slope[i] + rotation_v[i] * east[i])
            return out

        def lane_tile(i):
            return slice(i * LANES, (i + 1) * LANES)

        def averaged(fields):
            previous = fields
            current = [[0.5 * x for x in field] for field in applied(*fields)]

            def put_limbs(field, k, i, below, above):
                high, low = split(jnp.concatenate([below, above]))
                for at, limb in ((0, high), (group, low), (2 * group, high)):
                    limbs[field, at + k * SUBLANES : at + (k + 2) * SUBLANES, lane_tile(i)] = limb

            def store(k, lower, upper):
                for field in range(3):
                    for i in range(V):
                        below = lower[field][i]
                        above = upper[field][i] if upper else jnp.zeros_like(below)
                        put_limbs(field, k, i, below, above)
                        if field > 0:
                            put_limbs(field + 2, k, i, lon_diff(below), lon_diff(above) if upper else above)

            store(0, previous, current)
            for k in range(2, TERMS):
                step = applied(*current)
                previous, current = current, [[step[f][i] + previous[f][i] for i in range(V)] for f in range(3)]
                if k % 2 == 1:
                    store(k - 1, previous, current)
                elif k == DEG:
                    store(k, current, None)
            for field in range(5):
                waves[field] = jnp.dot(forward_m, limbs[field], preferred_element_type=jnp.float32)

            pair = 2 * SUBLANES
            half_rows = samples * SUBLANES

            def advect(j, carry):
                at = pl.multiple_of(j * pair, pair)
                height, east, north, east_lon, north_lon = [
                    [waves[f, pl.ds(at, pair), lane_tile(i)].reshape(2, SUBLANES, LANES) for i in range(V)] for f in range(5)
                ]
                flux = lat_diffs([height[i] * north[i] for i in range(V)])
                east_lat, north_lat = lat_diffs(east), lat_diffs(north)
                for i in range(V):
                    values = (
                        lon_diff(height[i] * east[i]) + flux[i],
                        east[i] * east_lon[i] + north[i] * east_lat[i],
                        east[i] * north_lon[i] + north[i] * north_lat[i],
                    )
                    for f in range(3):
                        high, low = split(values[f].reshape(pair, LANES))
                        pulled[f, pl.ds(at, pair), lane_tile(i)] = high
                        pulled[f, pl.ds(pl.multiple_of(half_rows + at, pair), pair), lane_tile(i)] = low
                return carry

            lax.fori_loop(0, samples // 2, advect, 0, unroll=unrolled)

            for field in range(3):
                sums[field] = jnp.dot(back_both, pulled[field], preferred_element_type=jnp.float32)

            def term(k):
                low = group + k * SUBLANES
                return [
                    [
                        sums[f, k * SUBLANES : (k + 1) * SUBLANES, lane_tile(i)] + sums[f, low : low + SUBLANES, lane_tile(i)]
                        for i in range(V)
                    ]
                    for f in range(3)
                ]

            after, now = None, term(DEG)
            for k in reversed(range(1, DEG)):
                step, own = applied(*now), term(k)
                following = [
                    [own[f][i] + step[f][i] + (after[f][i] if after is not None else 0.0) for i in range(V)] for f in range(3)
                ]
                after, now = now, following
            step, own = applied(*now), term(0)
            return [[own[f][i] + after[f][i] + 0.5 * step[f][i] for i in range(V)] for f in range(3)]

        first = averaged(start_state)
        middle = [[start_state[f][i] + time_step * first[f][i] for i in range(V)] for f in range(3)]
        second = averaged(middle)

        for field in range(3):
            factor = 0.5 * radius_scale if field == 0 else 0.5
            for i in range(V):
                out_message[row_slice(field, i), :] = factor * (first[field][i] + second[field][i])

        for_others(count, lambda tile: out_exchange(tile).start())
        mine_out = pl.ds(pl.multiple_of(mine_tile * size, SUBLANES), size)
        out_received[mine_out] = out_message[mine]
        if lats > 1:
            coef_all.wait_send()

    pl.semaphore_wait(barrier, tiles - computes.astype(jnp.int32))
    for_tiles_back(lambda tile: exchange(tile).start())

    @pl.when(computes)
    def _():
        compute()
        all_of(message, tiles - 1, size, send_sem, recv_sem).wait_send()
        all_of(out_received, tiles - 1, size, out_send, out_recv).wait_recv()

    @pl.when(jnp.logical_not(computes))
    def _():
        all_of(message, tiles, size, send_sem, recv_sem).wait_send()
        all_of(out_received, tiles, size, out_send, out_recv).wait_recv()

    starts = [tile * nlon // tiles for tile in range(tiles)] + [nlon]
    for t in range(lane_tiles):
        total = None
        for tile in range(tiles):
            if starts[tile] < (t + 1) * LANES and starts[tile + 1] > t * LANES:
                got = out_received[tile * size : (tile + 1) * size]
                total = got if total is None else jnp.where(lane >= starts[tile] - t * LANES, got, total)
        for field in range(3):
            at = slice(t * LANES, (t + 1) * LANES)
            piece = total[field * share : (field + 1) * share]
            tend_out[field, :, at] = piece
            next_out[field, :, at] = state[field, :, at] + time_step * piece

    @pl.when(computes)
    def _():
        all_of(out_message, count - 1, size, out_send, out_recv).wait_send()


def finish(next_in, tend_in, next_out, tend_out, sems):
    copies = [
        pltpu.make_async_copy(next_in, next_out, sems.at[0]),
        pltpu.make_async_copy(tend_in, tend_out, sems.at[1]),
    ]
    for copy in copies:
        copy.start()
    for copy in copies:
        copy.wait()


def per_device(phases, lats, nlat, state_now, ocean_depth, coriolis, phase_times, phase_weights):
    rows, share = ocean_depth.shape[0], state_now.shape[1]
    nlon = ocean_depth.shape[1]
    count = phases * lats
    size = message_rows(share)
    tiles = tiles_of(phases, lats, nlon)[1]
    wide = nlat // SUBLANES * LANES
    samples = phases
    group = 80
    vmem = pl.BlockSpec(memory_space=pltpu.VMEM)
    hbm = pl.BlockSpec(memory_space=pltpu.HBM)
    smem = pl.BlockSpec(memory_space=pltpu.SMEM)
    out = jax.ShapeDtypeStruct(state_now.shape, jnp.float32)
    f32, bf16 = jnp.float32, jnp.bfloat16
    scratch = [
        pltpu.VMEM(state_now.shape, f32),
        pltpu.VMEM(ocean_depth.shape, f32),
        pltpu.SMEM(coriolis.shape, f32),
        pltpu.VMEM((tiles * size, LANES), f32),
        pltpu.VMEM((count * size, LANES), f32),
        pltpu.VMEM((lats, 2 * rows, LANES), f32),
        pltpu.VMEM((lats * 2 * rows, LANES), f32),
        pltpu.VMEM((5, 3 * group, wide), bf16),
        pltpu.VMEM((5, samples * SUBLANES, wide), f32),
        pltpu.VMEM((3, 2 * samples * SUBLANES, wide), bf16),
        pltpu.VMEM((3, 2 * group, wide), f32),
        pltpu.VMEM((3, samples, LANES), f32),
        pltpu.VMEM((count * size, LANES), f32),
        pltpu.VMEM((tiles * size, LANES), f32),
        pltpu.SemaphoreType.DMA((3,)),
        pltpu.SemaphoreType.DMA((6,)),
    ]
    results = pl.pallas_call(
        functools.partial(kernel, phases, lats, nlat),
        out_shape=(out, out),
        in_specs=[hbm, hbm, hbm, smem, smem],
        out_specs=(vmem, vmem),
        scratch_shapes=scratch,
        compiler_params=pltpu.CompilerParams(
            collective_id=0, has_side_effects=True, vmem_limit_bytes=(60 if wide > 1024 else 32) * 1024 * 1024
        ),
    )(*[pltpu.with_memory_space_constraint(a, pltpu.HBM) for a in (state_now, ocean_depth, coriolis)], phase_times, phase_weights)
    return pl.pallas_call(
        finish,
        out_shape=(out, out),
        in_specs=[vmem, vmem],
        out_specs=(hbm, hbm),
        scratch_shapes=[pltpu.SemaphoreType.DMA((2,))],
    )(*[pltpu.with_memory_space_constraint(a, pltpu.VMEM) for a in results])


def solution(mesh):
    placed = (P(None, ("lat", "phase"), None), P("lat", None), P("lat"), P("phase"), P("phase"))

    def step(state_now, ocean_depth, coriolis, phase_times, phase_weights):
        return jax.shard_map(
            functools.partial(per_device, mesh.shape["phase"], mesh.shape["lat"], state_now.shape[1]),
            mesh=mesh,
            in_specs=placed,
            out_specs=(P(None, ("lat", "phase"), None), P(None, ("lat", "phase"), None)),
            check_vma=False,
        )(state_now, ocean_depth, coriolis, phase_times, phase_weights)

    return step
```

```python
import functools

import jax
import jax.numpy as jnp
from jax import lax
from jax.experimental import pallas as pl
from jax.experimental.pallas import tpu as pltpu
from jax.sharding import PartitionSpec as P

DEG = 8
TERMS = DEG + 1
LANES = 128
SUBLANES = 8
ROWS_PER_LIMB = 80

radius_scale = 2.5
time_step = 0.5
series_terms = 20

HEIGHT_SCALE = 1.0 / radius_scale
DEPTH_SCALE = 1.0 / (radius_scale * radius_scale)
ROTATION_SCALE = 2.0 / radius_scale


def message_rows(share):
    return -(-(3 * share + 2) // SUBLANES) * SUBLANES


HALO = 4 * DEG + 2
COMPUTING = (0, 1, 2, 4, 5, 6, 8, 9, 10)


def tiles_of(phases, lats, nlon):
    number = min(phases, -(-nlon // ((LANES - 2 * HALO) * lats)))
    computing = COMPUTING[:number] if phases == 16 and number == len(COMPUTING) else tuple(range(number))
    return computing, number * lats


def window_of(tile, tiles, nlon):
    start = tile * nlon // tiles - HALO + nlon
    left = start // LANES % (nlon // LANES)
    return left, (left + 1) % (nlon // LANES), start % LANES


def split(values):
    high = values.astype(jnp.bfloat16)
    return high, (values - high.astype(jnp.float32)).astype(jnp.bfloat16)


def kernel(
    phases,
    lats,
    nlat,
    state_in,
    depth_in,
    coriolis_in,
    times,
    weights,
    next_out,
    tend_out,
    state,
    depth,
    coriolis,
    message,
    received,
    coef_message,
    coef,
    limbs,
    waves,
    pulled,
    sums,
    series_rows,
    out_message,
    out_received,
    input_sem,
    barrier_free_sems,
):
    share, nlon = state.shape[1], state.shape[2]
    rows = depth.shape[0]
    count = phases * lats
    computing, tiles = tiles_of(phases, lats, nlon)
    lane_tiles = nlon // LANES
    size = message_rows(share)
    V = nlat // SUBLANES
    group = 80
    phase, lat = lax.axis_index("phase"), lax.axis_index("lat")
    me = lat * phases + phase
    place = phase * lats + lat
    rank = sum(jnp.where(phase == other, at, 0) for at, other in enumerate(computing))
    computes = functools.reduce(jnp.logical_or, [phase == other for other in computing])
    mine_tile = jnp.where(computes, rank * lats + lat, tiles)
    send_sem, recv_sem, coef_send, coef_recv, out_send, out_recv = [barrier_free_sems.at[i] for i in range(6)]

    unrolled = count <= 32

    def for_steps(start, stop, fn):
        if unrolled:
            for step in range(start, stop):
                fn(step)
        else:

            def body(step, carry):
                fn(step)
                return carry

            lax.fori_loop(start, stop, body, 0)

    def device(place):
        return {"phase": place // lats, "lat": place % lats}

    def for_others(stop, fn):
        def one(tile):
            pl.when(place != tile)(lambda: fn(tile))

        for_steps(0, stop, one)

    def for_tiles_back(fn):
        def one(back):
            tile = tiles - 1 - back
            pl.when(mine_tile != tile)(lambda: fn(tile))

        for back in range(tiles):
            one(back)

    barrier = pltpu.get_barrier_semaphore()

    @pl.when(computes)
    def _():
        for_others(count, lambda tile: pl.semaphore_signal(barrier, inc=1, device_id=device(tile)))

    pairs = ((state_in, state), (coriolis_in, coriolis), (depth_in, depth))
    copies = [pltpu.make_async_copy(source, target, input_sem.at[i]) for i, (source, target) in enumerate(pairs)]
    copies[0].start()

    @pl.when(computes)
    def _():
        copies[1].start()
        copies[2].start()

    lane = lax.broadcasted_iota(jnp.int32, (SUBLANES, LANES), 1)
    sub = lax.broadcasted_iota(jnp.int32, (SUBLANES, LANES), 0)
    degree = lane // SUBLANES

    half = jnp.full((SUBLANES, LANES), times[0] * 0.5, jnp.float32)
    weight = jnp.full((SUBLANES, LANES), weights[0], jnp.float32)
    square = half * half
    degree_f = degree.astype(jnp.float32)
    series = jnp.ones_like(half)
    for m in reversed(range(1, series_terms)):
        series = 1.0 - series * square * (1.0 / (m * (degree_f + float(m))))
    power = jnp.ones_like(half)
    scale = jnp.where(degree == 0, 1.0, 0.0)
    for k in range(1, TERMS):
        power = power * (half * (1.0 / k))
        scale = jnp.where(degree == k, 2.0 * power, scale)
    value = series * scale
    flipped = jnp.where(lax.rem(degree, 2) == 0, value, -value)
    coef_rows = jnp.where(sub == 3 * share, flipped, jnp.where(sub == 3 * share + 1, (-0.5 * weight) * value, 0.0))

    copies[0].wait()
    pieces = []
    for t in range(lane_tiles):
        at = slice(t * LANES, (t + 1) * LANES)
        full = coef_rows
        for field in range(3):
            piece = state[field, :, at]
            if field == 0:
                piece = piece * HEIGHT_SCALE
            for r in range(share):
                full = jnp.where(sub == field * share + r, piece[r : r + 1], full)
        pieces.append(full)

    for tile in range(tiles):
        left, right, edge = window_of(tile, tiles, nlon)
        message[tile * size : (tile + 1) * size] = jnp.where(lane >= edge, pieces[left], pieces[right])

    mine = pl.ds(pl.multiple_of(me * size, SUBLANES), size)

    own_coef = pl.ds(pl.multiple_of(lat * (2 * rows), SUBLANES), 2 * rows)

    def exchange(tile):
        return pltpu.make_async_remote_copy(
            src_ref=message.at[pl.ds(tile * size, size)],
            dst_ref=received.at[mine],
            send_sem=send_sem,
            recv_sem=recv_sem,
            device_id={"phase": computing[tile // lats], "lat": tile % lats},
        )

    def coef_exchange(step):
        return pltpu.make_async_remote_copy(
            src_ref=coef_message.at[step],
            dst_ref=coef.at[own_coef],
            send_sem=coef_send,
            recv_sem=coef_recv,
            device_id={"lat": lax.rem(lat + step, lats)},
        )

    def owner_rows(tile):
        return pl.ds(pl.multiple_of((tile % lats * phases + tile // lats) * size, SUBLANES), size)

    def out_exchange(tile):
        return pltpu.make_async_remote_copy(
            src_ref=out_message.at[owner_rows(tile)],
            dst_ref=out_received.at[pl.ds(pl.multiple_of(mine_tile * size, SUBLANES), size)],
            send_sem=out_send,
            recv_sem=out_recv,
            device_id=device(tile),
        )

    def all_of(array, number, length, send, recv):
        part = array.at[pl.ds(0, number * length)]
        return pltpu.make_async_remote_copy(
            src_ref=part, dst_ref=part, send_sem=send, recv_sem=recv, device_id=device(0)
        )

    def compute():
        received[mine] = message[pl.ds(pl.multiple_of(mine_tile * size, SUBLANES), size)]
        copies[1].wait()
        copies[2].wait()
        lane_wide = lax.broadcasted_iota(jnp.int32, (rows, LANES), 1)
        for row in range(rows):
            coef_message[0, rows + row : rows + row + 1] = jnp.full((1, LANES), coriolis[row] * ROTATION_SCALE, jnp.float32)
        for step in range(lats):
            target = lax.rem(lat + step, lats)
            left, right, edge = window_of(rank * lats + target, tiles, nlon)
            left = depth[:, pl.ds(pl.multiple_of(left * LANES, LANES), LANES)]
            right = depth[:, pl.ds(pl.multiple_of(right * LANES, LANES), LANES)]
            coef_message[step, 0:rows] = jnp.where(lane_wide >= edge, left, right) * DEPTH_SCALE
            if step > 0:
                coef_message[step, rows : 2 * rows] = coef_message[0, rows : 2 * rows]

        for step in range(1, lats):
            coef_exchange(step).start()
        coef[own_coef] = coef_message[0]

        if lats > 1:
            coef_all = all_of(coef, lats - 1, 2 * rows, coef_send, coef_recv)
            coef_all.wait_recv()

        stride = V // share * size

        def row_slice(field, i):
            return pl.ds(i // share * size + field * share + i % share, SUBLANES, stride)

        per = rows // V
        depth_v, rotation_v = [], []
        for i in range(V):
            both = []
            for which in range(2):
                parts = [coef[pl.ds(l * 2 * rows + which * rows + i, per, V), :] for l in range(lats)]
                both.append(jnp.concatenate(parts, axis=0) if lats > 1 else parts[0])
            depth_v.append(both[0])
            rotation_v.append(both[1])

        all_of(received, count - 1, size, send_sem, recv_sem).wait_recv()
        start_state = [[received[row_slice(field, i), :] for i in range(V)] for field in range(3)]

        diagonal = lax.rem(lane, SUBLANES) == sub
        samples = phases
        lane_s = lax.broadcasted_iota(jnp.int32, (samples, LANES), 1)
        value = received[pl.ds(3 * share, samples, size), :]
        high = value.astype(jnp.bfloat16).astype(jnp.float32)
        moved = pltpu.roll(high, group, 1)
        series_rows[0] = jnp.where(lane_s < group, high, moved)
        low = pltpu.roll(value - high, 2 * group - LANES, 1)
        series_rows[1] = jnp.where(lane_s < 2 * group - LANES, moved, low)
        series_rows[2] = received[pl.ds(3 * share + 1, samples, size), :]

        def spread(which):
            rows_of = [jnp.broadcast_to(series_rows[which, s : s + 1, :], (SUBLANES, LANES)) for s in range(samples)]
            return jnp.concatenate([jnp.where(diagonal, row, 0.0) for row in rows_of])

        forward_m = jnp.concatenate([spread(0).astype(jnp.bfloat16), spread(1).astype(jnp.bfloat16)], axis=1)[:, : 3 * group]
        back = jnp.transpose(spread(2))[:group]
        back_high, back_low = split(back)
        back_both = jnp.concatenate(
            [jnp.concatenate([back_high, back_high], axis=1), jnp.concatenate([back_low, jnp.zeros_like(back_low)], axis=1)]
        )

        def lon_diff(x):
            axis = x.ndim - 1
            return pltpu.roll(x, LANES - 1, axis) - pltpu.roll(x, 1, axis)

        def lat_diffs(xs):
            axis = xs[0].ndim - 2
            place = lax.broadcasted_iota(jnp.int32, xs[0].shape, axis)
            before = jnp.where(place == 0, 0.0, pltpu.roll(xs[-1], 1, axis))
            after = jnp.where(place == SUBLANES - 1, 0.0, pltpu.roll(xs[0], SUBLANES - 1, axis))
            return [(xs[i + 1] if i < V - 1 else after) - (xs[i - 1] if i > 0 else before) for i in range(V)]

        def applied(height, east, north):
            flux = lat_diffs([depth_v[i] * north[i] for i in range(V)])
            slope = lat_diffs(height)
            out = [[], [], []]
            for i in range(V):
                out[0].append(lon_diff(depth_v[i] * east[i]) + flux[i])
                out[1].append(lon_diff(height[i]) - rotation_v[i] * north[i])
                out[2].append(slope[i] + rotation_v[i] * east[i])
            return out

        def lane_tile(i):
            return slice(i * LANES, (i + 1) * LANES)

        def averaged(fields):
            previous = fields
            current = [[0.5 * x for x in field] for field in applied(*fields)]

            def put_limbs(field, k, i, below, above):
                high, low = split(jnp.concatenate([below, above]))
                for at, limb in ((0, high), (group, low), (2 * group, high)):
                    limbs[field, at + k * SUBLANES : at + (k + 2) * SUBLANES, lane_tile(i)] = limb

            def store(k, lower, upper):
                for field in range(3):
                    for i in range(V):
                        below = lower[field][i]
                        above = upper[field][i] if upper else jnp.zeros_like(below)
                        put_limbs(field, k, i, below, above)
                        if field > 0:
                            put_limbs(field + 2, k, i, lon_diff(below), lon_diff(above) if upper else above)

            store(0, previous, current)
            for k in range(2, TERMS):
                step = applied(*current)
                previous, current = current, [[step[f][i] + previous[f][i] for i in range(V)] for f in range(3)]
                if k % 2 == 1:
                    store(k - 1, previous, current)
                elif k == DEG:
                    store(k, current, None)
            for field in range(5):
                waves[field] = jnp.dot(forward_m, limbs[field], preferred_element_type=jnp.float32)

            pair = 2 * SUBLANES
            half_rows = samples * SUBLANES

            def advect(j, carry):
                at = pl.multiple_of(j * pair, pair)
                height, east, north, east_lon, north_lon = [
                    [waves[f, pl.ds(at, pair), lane_tile(i)].reshape(2, SUBLANES, LANES) for i in range(V)] for f in range(5)
                ]
                flux = lat_diffs([height[i] * north[i] for i in range(V)])
                east_lat, north_lat = lat_diffs(east), lat_diffs(north)
                for i in range(V):
                    values = (
                        lon_diff(height[i] * east[i]) + flux[i],
                        east[i] * east_lon[i] + north[i] * east_lat[i],
                        east[i] * north_lon[i] + north[i] * north_lat[i],
                    )
                    for f in range(3):
                        high, low = split(values[f].reshape(pair, LANES))
                        pulled[f, pl.ds(at, pair), lane_tile(i)] = high
                        pulled[f, pl.ds(pl.multiple_of(half_rows + at, pair), pair), lane_tile(i)] = low
                return carry

            lax.fori_loop(0, samples // 2, advect, 0, unroll=unrolled)

            for field in range(3):
                sums[field] = jnp.dot(back_both, pulled[field], preferred_element_type=jnp.float32)

            def term(k):
                low = group + k * SUBLANES
                return [
                    [
                        sums[f, k * SUBLANES : (k + 1) * SUBLANES, lane_tile(i)] + sums[f, low : low + SUBLANES, lane_tile(i)]
                        for i in range(V)
                    ]
                    for f in range(3)
                ]

            after, now = None, term(DEG)
            for k in reversed(range(1, DEG)):
                step, own = applied(*now), term(k)
                following = [
                    [own[f][i] + step[f][i] + (after[f][i] if after is not None else 0.0) for i in range(V)] for f in range(3)
                ]
                after, now = now, following
            step, own = applied(*now), term(0)
            return [[own[f][i] + after[f][i] + 0.5 * step[f][i] for i in range(V)] for f in range(3)]

        first = averaged(start_state)
        middle = [[start_state[f][i] + time_step * first[f][i] for i in range(V)] for f in range(3)]
        second = averaged(middle)

        for field in range(3):
            factor = 0.5 * radius_scale if field == 0 else 0.5
            for i in range(V):
                out_message[row_slice(field, i), :] = factor * (first[field][i] + second[field][i])

        for_others(count, lambda tile: out_exchange(tile).start())
        mine_out = pl.ds(pl.multiple_of(mine_tile * size, SUBLANES), size)
        out_received[mine_out] = out_message[mine]
        if lats > 1:
            coef_all.wait_send()

    pl.semaphore_wait(barrier, tiles - computes.astype(jnp.int32))
    for_tiles_back(lambda tile: exchange(tile).start())

    @pl.when(computes)
    def _():
        compute()
        all_of(message, tiles - 1, size, send_sem, recv_sem).wait_send()
        all_of(out_received, tiles - 1, size, out_send, out_recv).wait_recv()

    @pl.when(jnp.logical_not(computes))
    def _():
        all_of(message, tiles, size, send_sem, recv_sem).wait_send()
        all_of(out_received, tiles, size, out_send, out_recv).wait_recv()

    starts = [tile * nlon // tiles for tile in range(tiles)] + [nlon]
    for t in range(lane_tiles):
        total = None
        for tile in range(tiles):
            if starts[tile] < (t + 1) * LANES and starts[tile + 1] > t * LANES:
                got = out_received[tile * size : (tile + 1) * size]
                total = got if total is None else jnp.where(lane >= starts[tile] - t * LANES, got, total)
        for field in range(3):
            at = slice(t * LANES, (t + 1) * LANES)
            piece = total[field * share : (field + 1) * share]
            tend_out[field, :, at] = piece
            next_out[field, :, at] = state[field, :, at] + time_step * piece

    @pl.when(computes)
    def _():
        all_of(out_message, count - 1, size, out_send, out_recv).wait_send()


def finish(next_in, tend_in, next_out, tend_out, sems):
    copies = [
        pltpu.make_async_copy(next_in, next_out, sems.at[0]),
        pltpu.make_async_copy(tend_in, tend_out, sems.at[1]),
    ]
    for copy in copies:
        copy.start()
    for copy in copies:
        copy.wait()


def per_device(phases, lats, nlat, state_now, ocean_depth, coriolis, phase_times, phase_weights):
    rows, share = ocean_depth.shape[0], state_now.shape[1]
    nlon = ocean_depth.shape[1]
    count = phases * lats
    size = message_rows(share)
    tiles = tiles_of(phases, lats, nlon)[1]
    wide = nlat // SUBLANES * LANES
    samples = phases
    group = 80
    vmem = pl.BlockSpec(memory_space=pltpu.VMEM)
    hbm = pl.BlockSpec(memory_space=pltpu.HBM)
    smem = pl.BlockSpec(memory_space=pltpu.SMEM)
    out = jax.ShapeDtypeStruct(state_now.shape, jnp.float32)
    f32, bf16 = jnp.float32, jnp.bfloat16
    scratch = [
        pltpu.VMEM(state_now.shape, f32),
        pltpu.VMEM(ocean_depth.shape, f32),
        pltpu.SMEM(coriolis.shape, f32),
        pltpu.VMEM((tiles * size, LANES), f32),
        pltpu.VMEM((count * size, LANES), f32),
        pltpu.VMEM((lats, 2 * rows, LANES), f32),
        pltpu.VMEM((lats * 2 * rows, LANES), f32),
        pltpu.VMEM((5, 3 * group, wide), bf16),
        pltpu.VMEM((5, samples * SUBLANES, wide), f32),
        pltpu.VMEM((3, 2 * samples * SUBLANES, wide), bf16),
        pltpu.VMEM((3, 2 * group, wide), f32),
        pltpu.VMEM((3, samples, LANES), f32),
        pltpu.VMEM((count * size, LANES), f32),
        pltpu.VMEM((tiles * size, LANES), f32),
        pltpu.SemaphoreType.DMA((3,)),
        pltpu.SemaphoreType.DMA((6,)),
    ]
    results = pl.pallas_call(
        functools.partial(kernel, phases, lats, nlat),
        out_shape=(out, out),
        in_specs=[hbm, hbm, hbm, smem, smem],
        out_specs=(vmem, vmem),
        scratch_shapes=scratch,
        compiler_params=pltpu.CompilerParams(
            collective_id=0, has_side_effects=True, vmem_limit_bytes=(60 if wide > 1024 else 32) * 1024 * 1024
        ),
    )(*[pltpu.with_memory_space_constraint(a, pltpu.HBM) for a in (state_now, ocean_depth, coriolis)], phase_times, phase_weights)
    return pl.pallas_call(
        finish,
        out_shape=(out, out),
        in_specs=[vmem, vmem],
        out_specs=(hbm, hbm),
        scratch_shapes=[pltpu.SemaphoreType.DMA((2,))],
    )(*[pltpu.with_memory_space_constraint(a, pltpu.VMEM) for a in results])


def solution(mesh):
    placed = (P(None, ("lat", "phase"), None), P("lat", None), P("lat"), P("phase"), P("phase"))

    def step(state_now, ocean_depth, coriolis, phase_times, phase_weights):
        return jax.shard_map(
            functools.partial(per_device, mesh.shape["phase"], mesh.shape["lat"], state_now.shape[1]),
            mesh=mesh,
            in_specs=placed,
            out_specs=(P(None, ("lat", "phase"), None), P(None, ("lat", "phase"), None)),
            check_vma=False,
        )(state_now, ocean_depth, coriolis, phase_times, phase_weights)

    return step
```

```python
import functools

import jax
import jax.numpy as jnp
from jax import lax
from jax.experimental import pallas as pl
from jax.experimental.pallas import tpu as pltpu
from jax.sharding import PartitionSpec as P

DEG = 8
TERMS = DEG + 1
LANES = 128
SUBLANES = 8
ROWS_PER_LIMB = 80

radius_scale = 2.5
time_step = 0.5
series_terms = 20

HEIGHT_SCALE = 1.0 / radius_scale
DEPTH_SCALE = 1.0 / (radius_scale * radius_scale)
ROTATION_SCALE = 2.0 / radius_scale


def message_rows(share):
    return -(-(3 * share + 2) // SUBLANES) * SUBLANES


HALO = 4 * DEG + 2
COMPUTING = (0, 1, 2, 4, 5, 6, 8, 10, 3)


def tiles_of(phases, lats, nlon):
    number = min(phases, -(-nlon // ((LANES - 2 * HALO) * lats)))
    computing = COMPUTING[:number] if phases == 16 and number == len(COMPUTING) else tuple(range(number))
    return computing, number * lats


def window_of(tile, tiles, nlon):
    start = tile * nlon // tiles - HALO + nlon
    left = start // LANES % (nlon // LANES)
    return left, (left + 1) % (nlon // LANES), start % LANES


def split(values):
    high = values.astype(jnp.bfloat16)
    return high, (values - high.astype(jnp.float32)).astype(jnp.bfloat16)


def kernel(
    phases,
    lats,
    nlat,
    state_in,
    depth_in,
    coriolis_in,
    times,
    weights,
    next_out,
    tend_out,
    state,
    depth,
    coriolis,
    message,
    received,
    coef_message,
    coef,
    limbs,
    waves,
    pulled,
    sums,
    series_rows,
    out_message,
    out_received,
    input_sem,
    barrier_free_sems,
):
    share, nlon = state.shape[1], state.shape[2]
    rows = depth.shape[0]
    count = phases * lats
    computing, tiles = tiles_of(phases, lats, nlon)
    lane_tiles = nlon // LANES
    size = message_rows(share)
    V = nlat // SUBLANES
    group = 80
    phase, lat = lax.axis_index("phase"), lax.axis_index("lat")
    me = lat * phases + phase
    place = phase * lats + lat
    rank = sum(jnp.where(phase == other, at, 0) for at, other in enumerate(computing))
    computes = functools.reduce(jnp.logical_or, [phase == other for other in computing])
    mine_tile = jnp.where(computes, rank * lats + lat, tiles)
    send_sem, recv_sem, coef_send, coef_recv, out_send, out_recv = [barrier_free_sems.at[i] for i in range(6)]

    unrolled = count <= 32

    def for_steps(start, stop, fn):
        if unrolled:
            for step in range(start, stop):
                fn(step)
        else:

            def body(step, carry):
                fn(step)
                return carry

            lax.fori_loop(start, stop, body, 0)

    def device(place):
        return {"phase": place // lats, "lat": place % lats}

    def for_others(stop, fn):
        def one(tile):
            pl.when(place != tile)(lambda: fn(tile))

        for_steps(0, stop, one)

    def for_tiles_back(fn):
        def one(back):
            tile = tiles - 1 - back
            pl.when(mine_tile != tile)(lambda: fn(tile))

        for back in range(tiles):
            one(back)

    barrier = pltpu.get_barrier_semaphore()

    @pl.when(computes)
    def _():
        for_others(count, lambda tile: pl.semaphore_signal(barrier, inc=1, device_id=device(tile)))

    pairs = ((state_in, state), (coriolis_in, coriolis), (depth_in, depth))
    copies = [pltpu.make_async_copy(source, target, input_sem.at[i]) for i, (source, target) in enumerate(pairs)]
    copies[0].start()

    @pl.when(computes)
    def _():
        copies[1].start()
        copies[2].start()

    lane = lax.broadcasted_iota(jnp.int32, (SUBLANES, LANES), 1)
    sub = lax.broadcasted_iota(jnp.int32, (SUBLANES, LANES), 0)
    degree = lane // SUBLANES

    half = jnp.full((SUBLANES, LANES), times[0] * 0.5, jnp.float32)
    weight = jnp.full((SUBLANES, LANES), weights[0], jnp.float32)
    square = half * half
    degree_f = degree.astype(jnp.float32)
    series = jnp.ones_like(half)
    for m in reversed(range(1, series_terms)):
        series = 1.0 - series * square * (1.0 / (m * (degree_f + float(m))))
    power = jnp.ones_like(half)
    scale = jnp.where(degree == 0, 1.0, 0.0)
    for k in range(1, TERMS):
        power = power * (half * (1.0 / k))
        scale = jnp.where(degree == k, 2.0 * power, scale)
    value = series * scale
    flipped = jnp.where(lax.rem(degree, 2) == 0, value, -value)
    coef_rows = jnp.where(sub == 3 * share, flipped, jnp.where(sub == 3 * share + 1, (-0.5 * weight) * value, 0.0))

    copies[0].wait()
    pieces = []
    for t in range(lane_tiles):
        at = slice(t * LANES, (t + 1) * LANES)
        full = coef_rows
        for field in range(3):
            piece = state[field, :, at]
            if field == 0:
                piece = piece * HEIGHT_SCALE
            for r in range(share):
                full = jnp.where(sub == field * share + r, piece[r : r + 1], full)
        pieces.append(full)

    for tile in range(tiles):
        left, right, edge = window_of(tile, tiles, nlon)
        message[tile * size : (tile + 1) * size] = jnp.where(lane >= edge, pieces[left], pieces[right])

    mine = pl.ds(pl.multiple_of(me * size, SUBLANES), size)

    own_coef = pl.ds(pl.multiple_of(lat * (2 * rows), SUBLANES), 2 * rows)

    def exchange(tile):
        return pltpu.make_async_remote_copy(
            src_ref=message.at[pl.ds(tile * size, size)],
            dst_ref=received.at[mine],
            send_sem=send_sem,
            recv_sem=recv_sem,
            device_id={"phase": computing[tile // lats], "lat": tile % lats},
        )

    def coef_exchange(step):
        return pltpu.make_async_remote_copy(
            src_ref=coef_message.at[step],
            dst_ref=coef.at[own_coef],
            send_sem=coef_send,
            recv_sem=coef_recv,
            device_id={"lat": lax.rem(lat + step, lats)},
        )

    def owner_rows(tile):
        return pl.ds(pl.multiple_of((tile % lats * phases + tile // lats) * size, SUBLANES), size)

    def out_exchange(tile):
        return pltpu.make_async_remote_copy(
            src_ref=out_message.at[owner_rows(tile)],
            dst_ref=out_received.at[pl.ds(pl.multiple_of(mine_tile * size, SUBLANES), size)],
            send_sem=out_send,
            recv_sem=out_recv,
            device_id=device(tile),
        )

    def all_of(array, number, length, send, recv):
        part = array.at[pl.ds(0, number * length)]
        return pltpu.make_async_remote_copy(
            src_ref=part, dst_ref=part, send_sem=send, recv_sem=recv, device_id=device(0)
        )

    def compute():
        received[mine] = message[pl.ds(pl.multiple_of(mine_tile * size, SUBLANES), size)]
        copies[1].wait()
        copies[2].wait()
        lane_wide = lax.broadcasted_iota(jnp.int32, (rows, LANES), 1)
        for row in range(rows):
            coef_message[0, rows + row : rows + row + 1] = jnp.full((1, LANES), coriolis[row] * ROTATION_SCALE, jnp.float32)
        for step in range(lats):
            target = lax.rem(lat + step, lats)
            left, right, edge = window_of(rank * lats + target, tiles, nlon)
            left = depth[:, pl.ds(pl.multiple_of(left * LANES, LANES), LANES)]
            right = depth[:, pl.ds(pl.multiple_of(right * LANES, LANES), LANES)]
            coef_message[step, 0:rows] = jnp.where(lane_wide >= edge, left, right) * DEPTH_SCALE
            if step > 0:
                coef_message[step, rows : 2 * rows] = coef_message[0, rows : 2 * rows]

        for step in range(1, lats):
            coef_exchange(step).start()
        coef[own_coef] = coef_message[0]

        if lats > 1:
            coef_all = all_of(coef, lats - 1, 2 * rows, coef_send, coef_recv)
            coef_all.wait_recv()

        stride = V // share * size

        def row_slice(field, i):
            return pl.ds(i // share * size + field * share + i % share, SUBLANES, stride)

        per = rows // V
        depth_v, rotation_v = [], []
        for i in range(V):
            both = []
            for which in range(2):
                parts = [coef[pl.ds(l * 2 * rows + which * rows + i, per, V), :] for l in range(lats)]
                both.append(jnp.concatenate(parts, axis=0) if lats > 1 else parts[0])
            depth_v.append(both[0])
            rotation_v.append(both[1])

        all_of(received, count - 1, size, send_sem, recv_sem).wait_recv()
        start_state = [[received[row_slice(field, i), :] for i in range(V)] for field in range(3)]

        diagonal = lax.rem(lane, SUBLANES) == sub
        samples = phases
        lane_s = lax.broadcasted_iota(jnp.int32, (samples, LANES), 1)
        value = received[pl.ds(3 * share, samples, size), :]
        high = value.astype(jnp.bfloat16).astype(jnp.float32)
        moved = pltpu.roll(high, group, 1)
        series_rows[0] = jnp.where(lane_s < group, high, moved)
        low = pltpu.roll(value - high, 2 * group - LANES, 1)
        series_rows[1] = jnp.where(lane_s < 2 * group - LANES, moved, low)
        series_rows[2] = received[pl.ds(3 * share + 1, samples, size), :]

        def spread(which):
            rows_of = [jnp.broadcast_to(series_rows[which, s : s + 1, :], (SUBLANES, LANES)) for s in range(samples)]
            return jnp.concatenate([jnp.where(diagonal, row, 0.0) for row in rows_of])

        forward_m = jnp.concatenate([spread(0).astype(jnp.bfloat16), spread(1).astype(jnp.bfloat16)], axis=1)[:, : 3 * group]
        back = jnp.transpose(spread(2))[:group]
        back_high, back_low = split(back)
        back_both = jnp.concatenate(
            [jnp.concatenate([back_high, back_high], axis=1), jnp.concatenate([back_low, jnp.zeros_like(back_low)], axis=1)]
        )

        def lon_diff(x):
            axis = x.ndim - 1
            return pltpu.roll(x, LANES - 1, axis) - pltpu.roll(x, 1, axis)

        def lat_diffs(xs):
            axis = xs[0].ndim - 2
            place = lax.broadcasted_iota(jnp.int32, xs[0].shape, axis)
            before = jnp.where(place == 0, 0.0, pltpu.roll(xs[-1], 1, axis))
            after = jnp.where(place == SUBLANES - 1, 0.0, pltpu.roll(xs[0], SUBLANES - 1, axis))
            return [(xs[i + 1] if i < V - 1 else after) - (xs[i - 1] if i > 0 else before) for i in range(V)]

        def applied(height, east, north):
            flux = lat_diffs([depth_v[i] * north[i] for i in range(V)])
            slope = lat_diffs(height)
            out = [[], [], []]
            for i in range(V):
                out[0].append(lon_diff(depth_v[i] * east[i]) + flux[i])
                out[1].append(lon_diff(height[i]) - rotation_v[i] * north[i])
                out[2].append(slope[i] + rotation_v[i] * east[i])
            return out

        def lane_tile(i):
            return slice(i * LANES, (i + 1) * LANES)

        def averaged(fields):
            previous = fields
            current = [[0.5 * x for x in field] for field in applied(*fields)]

            def put_limbs(field, k, i, below, above):
                high, low = split(jnp.concatenate([below, above]))
                for at, limb in ((0, high), (group, low), (2 * group, high)):
                    limbs[field, at + k * SUBLANES : at + (k + 2) * SUBLANES, lane_tile(i)] = limb

            def store(k, lower, upper):
                for field in range(3):
                    for i in range(V):
                        below = lower[field][i]
                        above = upper[field][i] if upper else jnp.zeros_like(below)
                        put_limbs(field, k, i, below, above)
                        if field > 0:
                            put_limbs(field + 2, k, i, lon_diff(below), lon_diff(above) if upper else above)

            store(0, previous, current)
            for k in range(2, TERMS):
                step = applied(*current)
                previous, current = current, [[step[f][i] + previous[f][i] for i in range(V)] for f in range(3)]
                if k % 2 == 1:
                    store(k - 1, previous, current)
                elif k == DEG:
                    store(k, current, None)
            for field in range(5):
                waves[field] = jnp.dot(forward_m, limbs[field], preferred_element_type=jnp.float32)

            pair = 2 * SUBLANES
            half_rows = samples * SUBLANES

            def advect(j, carry):
                at = pl.multiple_of(j * pair, pair)
                height, east, north, east_lon, north_lon = [
                    [waves[f, pl.ds(at, pair), lane_tile(i)].reshape(2, SUBLANES, LANES) for i in range(V)] for f in range(5)
                ]
                flux = lat_diffs([height[i] * north[i] for i in range(V)])
                east_lat, north_lat = lat_diffs(east), lat_diffs(north)
                for i in range(V):
                    values = (
                        lon_diff(height[i] * east[i]) + flux[i],
                        east[i] * east_lon[i] + north[i] * east_lat[i],
                        east[i] * north_lon[i] + north[i] * north_lat[i],
                    )
                    for f in range(3):
                        high, low = split(values[f].reshape(pair, LANES))
                        pulled[f, pl.ds(at, pair), lane_tile(i)] = high
                        pulled[f, pl.ds(pl.multiple_of(half_rows + at, pair), pair), lane_tile(i)] = low
                return carry

            lax.fori_loop(0, samples // 2, advect, 0, unroll=unrolled)

            for field in range(3):
                sums[field] = jnp.dot(back_both, pulled[field], preferred_element_type=jnp.float32)

            def term(k):
                low = group + k * SUBLANES
                return [
                    [
                        sums[f, k * SUBLANES : (k + 1) * SUBLANES, lane_tile(i)] + sums[f, low : low + SUBLANES, lane_tile(i)]
                        for i in range(V)
                    ]
                    for f in range(3)
                ]

            after, now = None, term(DEG)
            for k in reversed(range(1, DEG)):
                step, own = applied(*now), term(k)
                following = [
                    [own[f][i] + step[f][i] + (after[f][i] if after is not None else 0.0) for i in range(V)] for f in range(3)
                ]
                after, now = now, following
            step, own = applied(*now), term(0)
            return [[own[f][i] + after[f][i] + 0.5 * step[f][i] for i in range(V)] for f in range(3)]

        first = averaged(start_state)
        middle = [[start_state[f][i] + time_step * first[f][i] for i in range(V)] for f in range(3)]
        second = averaged(middle)

        for field in range(3):
            factor = 0.5 * radius_scale if field == 0 else 0.5
            for i in range(V):
                out_message[row_slice(field, i), :] = factor * (first[field][i] + second[field][i])

        for_others(count, lambda tile: out_exchange(tile).start())
        mine_out = pl.ds(pl.multiple_of(mine_tile * size, SUBLANES), size)
        out_received[mine_out] = out_message[mine]
        if lats > 1:
            coef_all.wait_send()

    pl.semaphore_wait(barrier, tiles - computes.astype(jnp.int32))
    for_tiles_back(lambda tile: exchange(tile).start())

    @pl.when(computes)
    def _():
        compute()
        all_of(message, tiles - 1, size, send_sem, recv_sem).wait_send()
        all_of(out_received, tiles - 1, size, out_send, out_recv).wait_recv()

    @pl.when(jnp.logical_not(computes))
    def _():
        all_of(message, tiles, size, send_sem, recv_sem).wait_send()
        all_of(out_received, tiles, size, out_send, out_recv).wait_recv()

    starts = [tile * nlon // tiles for tile in range(tiles)] + [nlon]
    for t in range(lane_tiles):
        total = None
        for tile in range(tiles):
            if starts[tile] < (t + 1) * LANES and starts[tile + 1] > t * LANES:
                got = out_received[tile * size : (tile + 1) * size]
                total = got if total is None else jnp.where(lane >= starts[tile] - t * LANES, got, total)
        for field in range(3):
            at = slice(t * LANES, (t + 1) * LANES)
            piece = total[field * share : (field + 1) * share]
            tend_out[field, :, at] = piece
            next_out[field, :, at] = state[field, :, at] + time_step * piece

    @pl.when(computes)
    def _():
        all_of(out_message, count - 1, size, out_send, out_recv).wait_send()


def finish(next_in, tend_in, next_out, tend_out, sems):
    copies = [
        pltpu.make_async_copy(next_in, next_out, sems.at[0]),
        pltpu.make_async_copy(tend_in, tend_out, sems.at[1]),
    ]
    for copy in copies:
        copy.start()
    for copy in copies:
        copy.wait()


def per_device(phases, lats, nlat, state_now, ocean_depth, coriolis, phase_times, phase_weights):
    rows, share = ocean_depth.shape[0], state_now.shape[1]
    nlon = ocean_depth.shape[1]
    count = phases * lats
    size = message_rows(share)
    tiles = tiles_of(phases, lats, nlon)[1]
    wide = nlat // SUBLANES * LANES
    samples = phases
    group = 80
    vmem = pl.BlockSpec(memory_space=pltpu.VMEM)
    hbm = pl.BlockSpec(memory_space=pltpu.HBM)
    smem = pl.BlockSpec(memory_space=pltpu.SMEM)
    out = jax.ShapeDtypeStruct(state_now.shape, jnp.float32)
    f32, bf16 = jnp.float32, jnp.bfloat16
    scratch = [
        pltpu.VMEM(state_now.shape, f32),
        pltpu.VMEM(ocean_depth.shape, f32),
        pltpu.SMEM(coriolis.shape, f32),
        pltpu.VMEM((tiles * size, LANES), f32),
        pltpu.VMEM((count * size, LANES), f32),
        pltpu.VMEM((lats, 2 * rows, LANES), f32),
        pltpu.VMEM((lats * 2 * rows, LANES), f32),
        pltpu.VMEM((5, 3 * group, wide), bf16),
        pltpu.VMEM((5, samples * SUBLANES, wide), f32),
        pltpu.VMEM((3, 2 * samples * SUBLANES, wide), bf16),
        pltpu.VMEM((3, 2 * group, wide), f32),
        pltpu.VMEM((3, samples, LANES), f32),
        pltpu.VMEM((count * size, LANES), f32),
        pltpu.VMEM((tiles * size, LANES), f32),
        pltpu.SemaphoreType.DMA((3,)),
        pltpu.SemaphoreType.DMA((6,)),
    ]
    results = pl.pallas_call(
        functools.partial(kernel, phases, lats, nlat),
        out_shape=(out, out),
        in_specs=[hbm, hbm, hbm, smem, smem],
        out_specs=(vmem, vmem),
        scratch_shapes=scratch,
        compiler_params=pltpu.CompilerParams(
            collective_id=0, has_side_effects=True, vmem_limit_bytes=(60 if wide > 1024 else 32) * 1024 * 1024
        ),
    )(*[pltpu.with_memory_space_constraint(a, pltpu.HBM) for a in (state_now, ocean_depth, coriolis)], phase_times, phase_weights)
    return pl.pallas_call(
        finish,
        out_shape=(out, out),
        in_specs=[vmem, vmem],
        out_specs=(hbm, hbm),
        scratch_shapes=[pltpu.SemaphoreType.DMA((2,))],
    )(*[pltpu.with_memory_space_constraint(a, pltpu.VMEM) for a in results])


def solution(mesh):
    placed = (P(None, ("lat", "phase"), None), P("lat", None), P("lat"), P("phase"), P("phase"))

    def step(state_now, ocean_depth, coriolis, phase_times, phase_weights):
        return jax.shard_map(
            functools.partial(per_device, mesh.shape["phase"], mesh.shape["lat"], state_now.shape[1]),
            mesh=mesh,
            in_specs=placed,
            out_specs=(P(None, ("lat", "phase"), None), P(None, ("lat", "phase"), None)),
            check_vma=False,
        )(state_now, ocean_depth, coriolis, phase_times, phase_weights)

    return step
```
